32 devices in a mesh: orb: 4 (over y, x), grid: 8 (over z, core).
Axes of the slice: x: 2, y: 2, z: 4, core: 2. Of those that a mesh axis runs over, the one named last changes fastest.
Arguments:
- orbitals: float32 [32, 2048, 128], P('orb', 'grid'), may hold values from -6 to 6
- previous: float32 [32, 2048, 128], P('orb', 'grid'), may hold values from -6 to 6
- potential: float32 [32, 2048, 128], P('orb', 'grid'), may hold values from -3 to 3
- partners: int32 [32, 3], P(('orb', 'grid')), may hold values from 0 to 31, as said below
- offsets: int32 [32, 3, 3], P(('orb', 'grid')), may hold values from -16 to 16, as said below
Outputs:
- advanced: float32 [32, 2048, 128], P('orb', 'grid')
- exchange_force: float32 [32, 2048, 128], P('orb', 'grid')
The draws below stay inside these ranges and needn't reach their ends.
Inputs may be any that keep to these rules, and one draw needn't show every extreme that they name: `partners`: row n names three different orbitals among n + 1 to n + 4, counted modulo 32; so every intersecting pair is listed once, by its first orbital. There are integer box corners of the orbitals with offsets[n, q, :] = corner[partners[n, q]] - corner[n]; both ends of the range occur in every draw.
All inputs are finite; a program needn't handle non-finite values.
Results may differ from the reference program's by a relative error of at most 0.0003.
Values sent between devices are 32-bit elements; how exact they have to be, the bound alone decides.
A program may use at most 128 MiB of HBM per device.

```python
import math
import jax
import jax.numpy as jnp
from jax import lax

B = 64
SWEEPS = 4
AHEAD = 4
SHIFT = 16
ROWS = 2048
ORBITALS = 32


def pair_layout(key):
    base_key = jax.random.fold_in(key, 7)
    own_index = jnp.arange(ORBITALS, dtype=jnp.int32)[:, None]
    slot_index = jnp.arange(3, dtype=jnp.int32)[None, :]
    dropped = jax.random.randint(jax.random.fold_in(base_key, 1), (ORBITALS, 1), 0, AHEAD)
    distances = slot_index + 1 + (slot_index >= dropped).astype(jnp.int32)
    scores = jax.random.randint(jax.random.fold_in(base_key, 2), (ORBITALS, 3), 0, 4096) * 3 + slot_index
    ordering = jnp.argsort(scores, axis=1)
    distances = jnp.take_along_axis(distances, ordering, axis=1)
    partners = jnp.remainder(own_index + distances, ORBITALS).astype(jnp.int32)
    corners = jax.random.randint(jax.random.fold_in(base_key, 3), (ORBITALS, 3), 0, SHIFT + 1)
    anchor = jax.random.randint(jax.random.fold_in(base_key, 4), (), 0, ORBITALS)
    position = jnp.remainder(own_index[:, 0] - anchor, ORBITALS)
    pattern = jnp.where(position == 0, 0, jnp.where(position <= AHEAD, SHIFT, jnp.where(position <= 2 * AHEAD, 0, corners[:, 0])))
    corners = corners.at[:, 0].set(pattern.astype(jnp.int32))
    offsets = corners[partners] - corners[:, None, :]
    return (partners, offsets.astype(jnp.int32))


def draw_partners(key, part):
    partners, offsets = pair_layout(key)
    return partners


def draw_offsets(key, part):
    partners, offsets = pair_layout(key)
    return offsets


def level_of(own_key, shape, cuts, smallest, high):
    gain, own = 1.0, jax.random.fold_in(own_key, 6)
    for dim, parts in cuts:
        steps = jnp.exp(jax.random.uniform(jax.random.fold_in(own, dim), (parts,), jnp.float32, smallest / len(cuts), high / len(cuts)))
        gain = gain * jnp.repeat(steps, shape[dim] // parts).reshape([-1 if axis == dim else 1 for axis in range(len(shape))])
    return gain


def scatter_about(key, dims, deviation, reach, shards=(), kind=jnp.bfloat16):
    loudness = level_of(key, dims, shards, -0.22, 0.18) if shards else 1.0
    array = jax.random.normal(key, dims, jnp.float32) * deviation * loudness
    return jnp.minimum(jnp.maximum(array, -reach), reach).astype(kind)


def setup_inputs(seed: int = 0) -> dict:
    key_list = jax.random.split(jax.random.key(seed), 6)
    return {
        "orbitals": scatter_about(key_list[0], (ORBITALS, ROWS, 2 * B), 1.0, 6.0, ((0, 4), (1, 8)), jnp.float32),
        "previous": scatter_about(key_list[1], (ORBITALS, ROWS, 2 * B), 1.0, 6.0, ((0, 4), (1, 8)), jnp.float32),
        "potential": jnp.clip(jax.random.uniform(key_list[2], (ORBITALS, ROWS, 2 * B), jnp.float32, -3.0, 3.0) * level_of(key_list[2], (ORBITALS, ROWS, 2 * B), ((0, 4), (1, 8)), -0.4, 0.0), -3.0, 3.0),
        "partners": draw_partners(jax.random.fold_in(key_list[5], 71), 0),
        "offsets": draw_offsets(jax.random.fold_in(key_list[5], 71), 0),
    }


coulomb_factor = 4.0 * math.pi
exact_share = 0.25
verlet_factor = 0.05
lower_edge = 0.5
upper_edge = 16.0


def apply_operator(grid_field):
    leading = grid_field.ndim - 3
    padded = jnp.pad(grid_field, [(0, 0)] * leading + [(2, 2)] * 3)
    extent = grid_field.shape[-1]

    def displaced(axis_number, offset_cells):
        corner = [2, 2, 2]
        corner[axis_number] = 2 + offset_cells
        return padded[..., corner[0]:corner[0] + extent, corner[1]:corner[1] + extent, corner[2]:corner[2] + extent]

    nearest = displaced(0, 1) + displaced(0, -1) + displaced(1, 1) + displaced(1, -1) + displaced(2, 1) + displaced(2, -1)
    farther = displaced(0, 2) + displaced(0, -2) + displaced(1, 2) + displaced(1, -2) + displaced(2, 2) + displaced(2, -2)
    return 7.5 * grid_field - (4.0 / 3.0) * nearest + (1.0 / 12.0) * farther


def sweep_weights():
    centre = 0.5 * (upper_edge + lower_edge)
    radius = 0.5 * (upper_edge - lower_edge)
    ratio_sigma = centre / radius
    previous_rho = 1.0 / ratio_sigma
    weights = []
    for turn_index in range(SWEEPS - 1):
        current_rho = 1.0 / (2.0 * ratio_sigma - previous_rho)
        weights.append((current_rho * previous_rho, 2.0 * current_rho / radius))
        previous_rho = current_rho
    return centre, weights


def solve_potential(density):
    centre, weights = sweep_weights()
    residual = coulomb_factor * density
    direction = residual / centre
    solution = jnp.zeros_like(density)
    for turn_index in range(SWEEPS):
        solution = solution + direction
        residual = residual - apply_operator(direction)
        if turn_index + 1 < SWEEPS:
            keep_weight, residual_weight = weights[turn_index]
            direction = keep_weight * direction + residual_weight * residual
    return solution


def shift_box(one_box, offset, direction_sign):
    extent = one_box.shape[0]
    reach_cells = extent // 4
    padded = jnp.pad(one_box, reach_cells)
    corner = (reach_cells + direction_sign * offset).astype(jnp.int32)
    return lax.dynamic_slice(padded, (corner[0], corner[1], corner[2]), (extent, extent, extent))


def pair_terms(own_box, partner_boxes, pair_offsets):
    def single(partner_box, offset):
        moved_box = shift_box(partner_box, offset, 1)
        potential_box = solve_potential(own_box * moved_box)
        return potential_box * moved_box, shift_box(potential_box * own_box, offset, -1)

    own_terms, partner_terms = jax.vmap(single)(partner_boxes, pair_offsets)
    return jnp.sum(own_terms, axis=0), partner_terms


def reference(orbitals, previous, potential, partners, offsets):
    orbital_boxes = orbitals.reshape(ORBITALS, B, B, B)

    def visit_orbital(force_sum, orbital_index):
        chosen = partners[orbital_index]
        own_term, partner_term = pair_terms(orbital_boxes[orbital_index], orbital_boxes[chosen], offsets[orbital_index])
        force_sum = force_sum.at[orbital_index].add(own_term)
        force_sum = force_sum.at[chosen].add(partner_term)
        return force_sum, None

    force_sum, unused = lax.scan(visit_orbital, jnp.zeros_like(orbital_boxes), jnp.arange(ORBITALS, dtype=jnp.int32))
    exchange_force = (exact_share * force_sum).reshape(orbitals.shape)
    kinetic = (-0.5 * apply_operator(orbital_boxes)).reshape(orbitals.shape)
    acceleration = kinetic + exchange_force
    advanced = 2.0 * orbitals - previous + verlet_factor * (acceleration - potential * orbitals)
    return advanced, exchange_force
```

```python
import functools
import math

import jax
import jax.numpy as jnp
from jax import lax
from jax.experimental import pallas as pl
from jax.experimental.pallas import tpu as pltpu
from jax.sharding import PartitionSpec as P

B = 64
SWEEPS = 4
AHEAD = 4
SHIFT = 16
CORES = 2
LANES = 2 * B
PLANE_ROWS = B // 2
CHUNK = 4
ROW_PAD = SHIFT // 2
PADDED_ROWS = PLANE_ROWS + 3 * ROW_PAD

coulomb_factor = 4.0 * math.pi
exact_share = 0.25
verlet_factor = 0.05
lower_edge = 0.5
upper_edge = 16.0


def sweep_weights():
    centre = 0.5 * (upper_edge + lower_edge)
    radius = 0.5 * (upper_edge - lower_edge)
    ratio_sigma = centre / radius
    previous_rho = 1.0 / ratio_sigma
    weights = []
    for turn_index in range(SWEEPS - 1):
        current_rho = 1.0 / (2.0 * ratio_sigma - previous_rho)
        weights.append((current_rho * previous_rho, 2.0 * current_rho / radius))
        previous_rho = current_rho
    return (centre, weights)


def two_parts(x):
    high = x.astype(jnp.bfloat16)
    low = (x - high.astype(jnp.float32)).astype(jnp.bfloat16)
    return [high, low]


def stencil_matrix():
    source = lax.broadcasted_iota(jnp.int32, (2 * LANES, 2 * LANES), 0) % LANES
    column = lax.broadcasted_iota(jnp.int32, (2 * LANES, 2 * LANES), 1)
    target = column % LANES
    gap = jnp.abs(source - target)
    same = (source // B) == (target // B)
    inside = jnp.where(
        same,
        jnp.where(gap == 0, 90.0, jnp.where(gap == 1, -16.0, jnp.where(gap == 2, 1.0, 0.0))),
        jnp.where(gap == B, -16.0, 0.0),
    )
    across = jnp.where(gap == B, -16.0, 0.0)
    return jnp.where(column < LANES, inside, across).astype(jnp.bfloat16)


def operator12(window, matrix, count):
    rows = count * PLANE_ROWS

    def planes(start):
        return window[start : start + count].reshape(rows, LANES)

    x = planes(2)
    product = jnp.dot(
        jnp.concatenate(two_parts(x), axis=1), matrix, preferred_element_type=jnp.float32
    )
    inside, across = product[:, :LANES], product[:, LANES:]
    lane = lax.broadcasted_iota(jnp.int32, (rows, LANES), 1)
    row = lax.broadcasted_iota(jnp.int32, (rows, LANES), 0) % PLANE_ROWS
    downward = x + jnp.where(lane < B, across, 0.0)
    upward = x + jnp.where(lane >= B, across, 0.0)
    downward = jnp.where(row == 0, 0.0, pltpu.roll(downward, 1, 0))
    upward = jnp.where(row == PLANE_ROWS - 1, 0.0, pltpu.roll(upward, rows - 1, 0))
    beside = planes(0) + planes(4) - 16.0 * (planes(1) + planes(3))
    return inside + downward + upward + beside


def shift_matrix(odd, across):
    shape = (LANES, LANES)
    source = lax.broadcasted_iota(jnp.int32, shape, 0)
    target = lax.broadcasted_iota(jnp.int32, shape, 1)
    cells = (source % B) == (target % B) + across
    half = target // B + odd - source // B

    def one(wanted):
        return jnp.where(cells & (half == wanted), 1.0, 0.0).astype(jnp.bfloat16)

    here, following = one(0), one(2)
    return jnp.concatenate([here, here, following, following], axis=0)


def shifted(padded, first, offset, matrix):
    plane = SHIFT + first + offset[0]
    row = ROW_PAD + (offset[1] >> 1)
    rows = CHUNK * PLANE_ROWS
    here = padded[pl.ds(plane, CHUNK), pl.ds(row, PLANE_ROWS), :].reshape(rows, LANES)
    following = padded[pl.ds(plane, CHUNK), pl.ds(row + 1, PLANE_ROWS), :].reshape(rows, LANES)
    parts = jnp.concatenate(two_parts(here) + two_parts(following), axis=1)
    return jnp.dot(parts, matrix, preferred_element_type=jnp.float32)


def pair_kernel(
    chosen, offsets, mine, theirs, kept, passed,
    padded, own, moved, first, second, residual, total, own_force, stencil, mover,
):
    chips, _, depth = mine.shape[:3]
    core = lax.rem(lax.axis_index("grid"), CORES)
    chunks = B // CHUNK
    centre, weights = sweep_weights()
    shape3 = (CHUNK, PLANE_ROWS, LANES)

    stencil[...] = stencil_matrix()
    zero_plane = jnp.zeros((2, PLANE_ROWS, LANES), jnp.float32)
    for buffer in (first, second):
        buffer[0:2] = zero_plane
        buffer[B + 2 : B + 4] = zero_plane
    own_force[...] = jnp.zeros_like(own_force)
    kept[...] = jnp.zeros_like(kept)
    passed[...] = jnp.zeros_like(passed)

    @pl.loop(0, padded.shape[0])
    def _(plane):
        padded[plane] = jnp.zeros(padded.shape[1:], jnp.float32)

    def slab_start(chip, which):
        return (chip * CORES + which) * depth

    @pl.loop(0, chips)
    def _(chip):
        own[pl.ds(slab_start(chip, core), depth)] = mine[chip, core]
        own[pl.ds(slab_start(chip, 1 - core), depth)] = theirs[chip, 0]

    @pl.loop(0, chosen.shape[0])
    def _(pair):
        partner = chosen[pair]
        offset = [offsets[pair, axis] for axis in range(3)]
        inside_rows = pl.ds(ROW_PAD, PLANE_ROWS)

        @pl.loop(0, chips)
        def _(chip):
            padded[pl.ds(SHIFT + slab_start(chip, core), depth), inside_rows, :] = mine[
                chip, core + partner
            ]
            padded[pl.ds(SHIFT + slab_start(chip, 1 - core), depth), inside_rows, :] = theirs[
                chip, partner
            ]

        mover[...] = shift_matrix(offset[1] & 1, offset[2])

        @pl.loop(0, chunks)
        def _(chunk):
            at = pl.multiple_of(chunk * CHUNK, CHUNK)
            there = shifted(padded, at, offset, mover[...]).reshape(shape3)
            moved[pl.ds(at, CHUNK)] = there
            start = coulomb_factor * (own[pl.ds(at, CHUNK)] * there)
            residual[pl.ds(at, CHUNK)] = start
            direction = start * (1.0 / centre)
            first[pl.ds(at + 2, CHUNK)] = direction
            total[pl.ds(at, CHUNK)] = direction

        source, target = first, second
        for turn in range(SWEEPS - 1):
            keep_weight, residual_weight = weights[turn]
            last = turn == SWEEPS - 2

            @pl.loop(0, chunks)
            def _(chunk, source=source, target=target, keep=keep_weight, gain=residual_weight, last=last):
                at = pl.multiple_of(chunk * CHUNK, CHUNK)
                window = source[pl.ds(at, CHUNK + 4)]
                applied = operator12(window, stencil[...], CHUNK).reshape(shape3)
                left = residual[pl.ds(at, CHUNK)] - (1.0 / 12.0) * applied
                direction = keep * window[2 : CHUNK + 2] + gain * left
                solved = total[pl.ds(at, CHUNK)] + direction
                if last:
                    own_force[pl.ds(at, CHUNK)] += solved * moved[pl.ds(at, CHUNK)]
                    padded[pl.ds(SHIFT + at, CHUNK), inside_rows, :] = solved * own[pl.ds(at, CHUNK)]
                else:
                    residual[pl.ds(at, CHUNK)] = left
                    target[pl.ds(at + 2, CHUNK)] = direction
                    total[pl.ds(at, CHUNK)] = solved

            source, target = target, source

        back = [-part for part in offset]
        mover[...] = shift_matrix(back[1] & 1, back[2])

        @pl.loop(0, chunks)
        def _(chunk):
            at = pl.multiple_of(chunk * CHUNK, CHUNK)
            there = shifted(padded, at, back, mover[...]).reshape(shape3)
            total[pl.ds(at, CHUNK)] = exact_share * there

        @pl.loop(0, chips)
        def _(chip):
            kept[chip, core + partner] = total[pl.ds(slab_start(chip, core), depth)]
            passed[chip, partner] = total[pl.ds(slab_start(chip, 1 - core), depth)]

    @pl.loop(0, chips)
    def _(chip):
        kept[chip, core] = exact_share * own_force[pl.ds(slab_start(chip, core), depth)]
        passed[chip, 0] = exact_share * own_force[pl.ds(slab_start(chip, 1 - core), depth)]


def pair_forces(chosen, offsets, mine, theirs):
    box = (B, PLANE_ROWS, LANES)
    f32 = jnp.float32
    vmem = pl.BlockSpec(memory_space=pltpu.VMEM)
    smem = pl.BlockSpec(memory_space=pltpu.SMEM)
    return pl.pallas_call(
        pair_kernel,
        out_shape=(
            jax.ShapeDtypeStruct(mine.shape, f32),
            jax.ShapeDtypeStruct(theirs.shape, f32),
        ),
        in_specs=[smem, smem, vmem, vmem],
        out_specs=(vmem, vmem),
        scratch_shapes=[
            pltpu.VMEM((B + 2 * SHIFT, PADDED_ROWS, LANES), f32),
            pltpu.VMEM(box, f32),
            pltpu.VMEM(box, f32),
            pltpu.VMEM((B + 4, PLANE_ROWS, LANES), f32),
            pltpu.VMEM((B + 4, PLANE_ROWS, LANES), f32),
            pltpu.VMEM(box, f32),
            pltpu.VMEM(box, f32),
            pltpu.VMEM(box, f32),
            pltpu.VMEM((2 * LANES, 2 * LANES), jnp.bfloat16),
            pltpu.VMEM((4 * LANES, LANES), jnp.bfloat16),
        ],
        compiler_params=pltpu.CompilerParams(vmem_limit_bytes=56 << 20),
        name="pair_forces",
    )(chosen, offsets, mine, theirs)


def step_kernel(now, before, after, previous, potential, force, advanced):
    depth = now.shape[1]
    window = jnp.concatenate([before[0], now[0], after[0]], axis=0)
    size = math.gcd(depth, CHUNK)
    matrix = stencil_matrix()
    for at in range(0, depth, size):
        applied = operator12(window[at : at + size + 4], matrix, size)
        kinetic = (-0.5 / 12.0) * applied.reshape(size, PLANE_ROWS, LANES)
        part = slice(at, at + size)
        field = now[0, part]
        acceleration = kinetic + force[0, part]
        advanced[0, part] = (
            2.0 * field
            - previous[0, part]
            + verlet_factor * (acceleration - potential[0, part] * field)
        )


def verlet_step(now, before, after, previous, potential, force):
    count = now.shape[0]

    def spec(array):
        return pl.BlockSpec((1,) + array.shape[1:], lambda n: (n, 0, 0, 0))

    operands = (now, before, after, previous, potential, force)
    return pl.pallas_call(
        step_kernel,
        grid=(count,),
        out_shape=jax.ShapeDtypeStruct(now.shape, jnp.float32),
        in_specs=[spec(array) for array in operands],
        out_specs=spec(now),
        name="verlet_step",
    )(*operands)


def from_behind(array, axis, by):
    count = lax.axis_size(axis)
    return lax.ppermute(array, axis, [(i, (i + by) % count) for i in range(count)])


def neighbour_planes(planes):
    count = lax.axis_size("grid")
    depth = planes.shape[1]
    before, after = [], []
    for hop in range(1, -(-2 // depth) + 1):
        size = min(depth, 2 - (hop - 1) * depth)
        forward = [(i, i + hop) for i in range(count - hop)]
        backward = [(i + hop, i) for i in range(count - hop)]
        before.insert(0, lax.ppermute(planes[:, depth - size :], "grid", forward))
        after.append(lax.ppermute(planes[:, :size], "grid", backward))
    return jnp.concatenate(before, axis=1), jnp.concatenate(after, axis=1)


def local(orbitals, previous, potential, partners, offsets):
    slabs = lax.axis_size("grid")
    chips = slabs // CORES
    core = lax.rem(lax.axis_index("grid"), CORES)
    total_orbitals = lax.axis_size(("orb", "grid"))
    group, rows, width = orbitals.shape
    depth = rows // PLANE_ROWS
    planes = orbitals.reshape(group, depth, PLANE_ROWS, width)
    tail = planes.shape[1:]
    steps = AHEAD // CORES
    across = [[chip * CORES + c for chip in range(chips)] for c in range(CORES)]
    swap = [(i, i + 1 - 2 * (i % CORES)) for i in range(slabs)]

    upper = from_behind(planes[:AHEAD], "orb", -1)
    before, after = neighbour_planes(planes)
    blocks = jnp.concatenate([planes, upper], axis=0).reshape((chips + steps, CORES) + tail)
    windows = jnp.concatenate([blocks[s : s + chips] for s in range(steps + 1)], axis=1)
    mine = lax.all_to_all(
        windows, "grid", split_axis=0, concat_axis=0, axis_index_groups=across, tiled=True
    )
    wanted = lax.dynamic_slice_in_dim(mine, 1 - core, 1 + AHEAD, axis=1)
    theirs = lax.ppermute(wanted, "grid", swap)

    first_index = lax.axis_index(("orb", "grid"))
    chosen = jnp.remainder(partners - first_index, total_orbitals).reshape(-1)
    kept, passed = pair_forces(chosen, offsets[0], mine, theirs)

    received = lax.ppermute(passed, "grid", swap)
    summed = kept + lax.dynamic_update_slice_in_dim(
        jnp.zeros_like(kept), received, 1 - core, axis=1
    )
    returned = lax.all_to_all(
        summed, "grid", split_axis=0, concat_axis=0, axis_index_groups=across, tiled=True
    )
    returned = returned.reshape((chips, steps + 1, CORES) + tail)
    folded = sum(
        jnp.pad(returned[:, s], ((s, steps - s),) + ((0, 0),) * (len(tail) + 1))
        for s in range(steps + 1)
    ).reshape(((chips + steps) * CORES,) + tail)
    spilled = from_behind(folded[group:], "orb", 1)
    force = folded[:group] + jnp.pad(spilled, ((0, group - AHEAD),) + ((0, 0),) * len(tail))

    advanced = verlet_step(
        planes, before, after, previous.reshape(planes.shape), potential.reshape(planes.shape), force
    )
    return advanced.reshape(orbitals.shape), force.reshape(orbitals.shape)


def solution(mesh):
    in_specs = (
        P("orb", "grid", None),
        P("orb", "grid", None),
        P("orb", "grid", None),
        P(("orb", "grid"), None),
        P(("orb", "grid"), None, None),
    )
    out_specs = (P("orb", "grid", None), P("orb", "grid", None))
    return jax.shard_map(local, mesh=mesh, in_specs=in_specs, out_specs=out_specs, check_vma=False)
```

```python
import functools
import math

import jax
import jax.numpy as jnp
from jax import lax
from jax.experimental import pallas as pl
from jax.experimental.pallas import tpu as pltpu
from jax.sharding import PartitionSpec as P

B = 64
SWEEPS = 4
AHEAD = 4
SHIFT = 16
CORES = 2
LANES = 2 * B
PLANE_ROWS = B // 2
CHUNK = 16
ROW_PAD = SHIFT // 2
PADDED_ROWS = PLANE_ROWS + 3 * ROW_PAD

coulomb_factor = 4.0 * math.pi
exact_share = 0.25
verlet_factor = 0.05
lower_edge = 0.5
upper_edge = 16.0


def sweep_weights():
    centre = 0.5 * (upper_edge + lower_edge)
    radius = 0.5 * (upper_edge - lower_edge)
    ratio_sigma = centre / radius
    previous_rho = 1.0 / ratio_sigma
    weights = []
    for turn_index in range(SWEEPS - 1):
        current_rho = 1.0 / (2.0 * ratio_sigma - previous_rho)
        weights.append((current_rho * previous_rho, 2.0 * current_rho / radius))
        previous_rho = current_rho
    return (centre, weights)


def two_parts(x):
    high = x.astype(jnp.bfloat16)
    low = (x - high.astype(jnp.float32)).astype(jnp.bfloat16)
    return [high, low]


def stencil_matrix():
    source = lax.broadcasted_iota(jnp.int32, (2 * LANES, 2 * LANES), 0) % LANES
    column = lax.broadcasted_iota(jnp.int32, (2 * LANES, 2 * LANES), 1)
    target = column % LANES
    gap = jnp.abs(source - target)
    same = (source // B) == (target // B)
    inside = jnp.where(
        same,
        jnp.where(gap == 0, 90.0, jnp.where(gap == 1, -16.0, jnp.where(gap == 2, 1.0, 0.0))),
        jnp.where(gap == B, -16.0, 0.0),
    )
    across = jnp.where(gap == B, -16.0, 0.0)
    return jnp.where(column < LANES, inside, across).astype(jnp.bfloat16)


def operator12(window, matrix, count):
    rows = count * PLANE_ROWS

    def planes(start):
        return window[start : start + count].reshape(rows, LANES)

    x = planes(2)
    product = jnp.dot(
        jnp.concatenate(two_parts(x), axis=1), matrix, preferred_element_type=jnp.float32
    )
    inside, across = product[:, :LANES], product[:, LANES:]
    lane = lax.broadcasted_iota(jnp.int32, (rows, LANES), 1)
    row = lax.broadcasted_iota(jnp.int32, (rows, LANES), 0) % PLANE_ROWS
    downward = x + jnp.where(lane < B, across, 0.0)
    upward = x + jnp.where(lane >= B, across, 0.0)
    downward = jnp.where(row == 0, 0.0, pltpu.roll(downward, 1, 0))
    upward = jnp.where(row == PLANE_ROWS - 1, 0.0, pltpu.roll(upward, rows - 1, 0))
    beside = planes(0) + planes(4) - 16.0 * (planes(1) + planes(3))
    return inside + downward + upward + beside


def shift_matrix(odd, across):
    shape = (LANES, LANES)
    source = lax.broadcasted_iota(jnp.int32, shape, 0)
    target = lax.broadcasted_iota(jnp.int32, shape, 1)
    cells = (source % B) == (target % B) + across
    half = target // B + odd - source // B

    def one(wanted):
        return jnp.where(cells & (half == wanted), 1.0, 0.0).astype(jnp.bfloat16)

    here, following = one(0), one(2)
    return jnp.concatenate([here, here, following, following], axis=0)


def shifted(padded, first, offset, matrix):
    plane = SHIFT + first + offset[0]
    row = ROW_PAD + (offset[1] >> 1)
    rows = CHUNK * PLANE_ROWS
    here = padded[pl.ds(plane, CHUNK), pl.ds(row, PLANE_ROWS), :].reshape(rows, LANES)
    following = padded[pl.ds(plane, CHUNK), pl.ds(row + 1, PLANE_ROWS), :].reshape(rows, LANES)
    parts = jnp.concatenate(two_parts(here) + two_parts(following), axis=1)
    return jnp.dot(parts, matrix, preferred_element_type=jnp.float32)


def pair_kernel(
    chosen, offsets, mine, theirs, kept, passed,
    padded, own, moved, first, second, residual, total, own_force, stencil, mover,
):
    chips, _, depth = mine.shape[:3]
    core = lax.rem(lax.axis_index("grid"), CORES)
    chunks = B // CHUNK
    centre, weights = sweep_weights()
    shape3 = (CHUNK, PLANE_ROWS, LANES)

    stencil[...] = stencil_matrix()
    zero_plane = jnp.zeros((2, PLANE_ROWS, LANES), jnp.float32)
    for buffer in (first, second):
        buffer[0:2] = zero_plane
        buffer[B + 2 : B + 4] = zero_plane
    own_force[...] = jnp.zeros_like(own_force)
    kept[...] = jnp.zeros_like(kept)
    passed[...] = jnp.zeros_like(passed)

    @pl.loop(0, padded.shape[0])
    def _(plane):
        padded[plane] = jnp.zeros(padded.shape[1:], jnp.float32)

    def slab_start(chip, which):
        return (chip * CORES + which) * depth

    @pl.loop(0, chips)
    def _(chip):
        own[pl.ds(slab_start(chip, core), depth)] = mine[chip, core]
        own[pl.ds(slab_start(chip, 1 - core), depth)] = theirs[chip, 0]

    @pl.loop(0, chosen.shape[0])
    def _(pair):
        partner = chosen[pair]
        offset = [offsets[pair, axis] for axis in range(3)]
        inside_rows = pl.ds(ROW_PAD, PLANE_ROWS)

        @pl.loop(0, chips)
        def _(chip):
            padded[pl.ds(SHIFT + slab_start(chip, core), depth), inside_rows, :] = mine[
                chip, core + partner
            ]
            padded[pl.ds(SHIFT + slab_start(chip, 1 - core), depth), inside_rows, :] = theirs[
                chip, partner
            ]

        mover[...] = shift_matrix(offset[1] & 1, offset[2])

        @pl.loop(0, chunks)
        def _(chunk):
            at = pl.multiple_of(chunk * CHUNK, CHUNK)
            there = shifted(padded, at, offset, mover[...]).reshape(shape3)
            moved[pl.ds(at, CHUNK)] = there
            start = coulomb_factor * (own[pl.ds(at, CHUNK)] * there)
            residual[pl.ds(at, CHUNK)] = start
            direction = start * (1.0 / centre)
            first[pl.ds(at + 2, CHUNK)] = direction
            total[pl.ds(at, CHUNK)] = direction

        source, target = first, second
        for turn in range(SWEEPS - 1):
            keep_weight, residual_weight = weights[turn]
            last = turn == SWEEPS - 2

            @pl.loop(0, chunks)
            def _(chunk, source=source, target=target, keep=keep_weight, gain=residual_weight, last=last):
                at = pl.multiple_of(chunk * CHUNK, CHUNK)
                window = source[pl.ds(at, CHUNK + 4)]
                applied = operator12(window, stencil[...], CHUNK).reshape(shape3)
                left = residual[pl.ds(at, CHUNK)] - (1.0 / 12.0) * applied
                direction = keep * window[2 : CHUNK + 2] + gain * left
                solved = total[pl.ds(at, CHUNK)] + direction
                if last:
                    own_force[pl.ds(at, CHUNK)] += solved * moved[pl.ds(at, CHUNK)]
                    padded[pl.ds(SHIFT + at, CHUNK), inside_rows, :] = solved * own[pl.ds(at, CHUNK)]
                else:
                    residual[pl.ds(at, CHUNK)] = left
                    target[pl.ds(at + 2, CHUNK)] = direction
                    total[pl.ds(at, CHUNK)] = solved

            source, target = target, source

        back = [-part for part in offset]
        mover[...] = shift_matrix(back[1] & 1, back[2])

        @pl.loop(0, chunks)
        def _(chunk):
            at = pl.multiple_of(chunk * CHUNK, CHUNK)
            there = shifted(padded, at, back, mover[...]).reshape(shape3)
            total[pl.ds(at, CHUNK)] = exact_share * there

        @pl.loop(0, chips)
        def _(chip):
            kept[chip, core + partner] = total[pl.ds(slab_start(chip, core), depth)]
            passed[chip, partner] = total[pl.ds(slab_start(chip, 1 - core), depth)]

    @pl.loop(0, chips)
    def _(chip):
        kept[chip, core] = exact_share * own_force[pl.ds(slab_start(chip, core), depth)]
        passed[chip, 0] = exact_share * own_force[pl.ds(slab_start(chip, 1 - core), depth)]


def pair_forces(chosen, offsets, mine, theirs):
    box = (B, PLANE_ROWS, LANES)
    f32 = jnp.float32
    vmem = pl.BlockSpec(memory_space=pltpu.VMEM)
    smem = pl.BlockSpec(memory_space=pltpu.SMEM)
    return pl.pallas_call(
        pair_kernel,
        out_shape=(
            jax.ShapeDtypeStruct(mine.shape, f32),
            jax.ShapeDtypeStruct(theirs.shape, f32),
        ),
        in_specs=[smem, smem, vmem, vmem],
        out_specs=(vmem, vmem),
        scratch_shapes=[
            pltpu.VMEM((B + 2 * SHIFT, PADDED_ROWS, LANES), f32),
            pltpu.VMEM(box, f32),
            pltpu.VMEM(box, f32),
            pltpu.VMEM((B + 4, PLANE_ROWS, LANES), f32),
            pltpu.VMEM((B + 4, PLANE_ROWS, LANES), f32),
            pltpu.VMEM(box, f32),
            pltpu.VMEM(box, f32),
            pltpu.VMEM(box, f32),
            pltpu.VMEM((2 * LANES, 2 * LANES), jnp.bfloat16),
            pltpu.VMEM((4 * LANES, LANES), jnp.bfloat16),
        ],
        compiler_params=pltpu.CompilerParams(vmem_limit_bytes=56 << 20),
        name="pair_forces",
    )(chosen, offsets, mine, theirs)


def step_kernel(now, before, after, previous, potential, partial):
    depth = now.shape[1]
    window = jnp.concatenate([before[0], now[0], after[0]], axis=0)
    applied = operator12(window, stencil_matrix(), depth)
    kinetic = (-0.5 / 12.0) * applied.reshape(now.shape[1:])
    field = now[0]
    partial[0] = (
        2.0 * field - previous[0] + verlet_factor * (kinetic - potential[0] * field)
    )


def step_without_force(now, before, after, previous, potential):
    count = now.shape[0]

    def spec(array):
        return pl.BlockSpec((1,) + array.shape[1:], lambda n: (n, 0, 0, 0))

    operands = (now, before, after, previous, potential)
    return pl.pallas_call(
        step_kernel,
        grid=(count,),
        out_shape=jax.ShapeDtypeStruct(now.shape, jnp.float32),
        in_specs=[spec(array) for array in operands],
        out_specs=spec(now),
        cost_estimate=pl.CostEstimate(
            flops=40 * now.size, bytes_accessed=20 * now.size, transcendentals=0
        ),
        name="step_without_force",
    )(*operands)


def from_behind(array, axis, by):
    count = lax.axis_size(axis)
    return lax.ppermute(array, axis, [(i, (i + by) % count) for i in range(count)])


def neighbour_planes(planes):
    count = lax.axis_size("grid")
    depth = planes.shape[1]
    before, after = [], []
    for hop in range(1, -(-2 // depth) + 1):
        size = min(depth, 2 - (hop - 1) * depth)
        forward = [(i, i + hop) for i in range(count - hop)]
        backward = [(i + hop, i) for i in range(count - hop)]
        before.insert(0, lax.ppermute(planes[:, depth - size :], "grid", forward))
        after.append(lax.ppermute(planes[:, :size], "grid", backward))
    return jnp.concatenate(before, axis=1), jnp.concatenate(after, axis=1)


def local(orbitals, previous, potential, partners, offsets):
    slabs = lax.axis_size("grid")
    chips = slabs // CORES
    core = lax.rem(lax.axis_index("grid"), CORES)
    total_orbitals = lax.axis_size(("orb", "grid"))
    group, rows, width = orbitals.shape
    depth = rows // PLANE_ROWS
    planes = orbitals.reshape(group, depth, PLANE_ROWS, width)
    tail = planes.shape[1:]
    steps = AHEAD // CORES
    across = [[chip * CORES + c for chip in range(chips)] for c in range(CORES)]
    swap = [(i, i + 1 - 2 * (i % CORES)) for i in range(slabs)]

    upper = from_behind(planes[:AHEAD], "orb", -1)
    before, after = neighbour_planes(planes)
    blocks = jnp.concatenate([planes, upper], axis=0).reshape((chips + steps, CORES) + tail)

    def exchange(array):
        return lax.all_to_all(
            array, "grid", split_axis=0, concat_axis=0, axis_index_groups=across, tiled=True
        )

    own_group = exchange(planes.reshape((chips, CORES) + tail))
    ahead = exchange(
        jnp.concatenate([blocks[s : s + chips] for s in range(1, steps + 1)], axis=1)
    )
    mine = jnp.concatenate([own_group, ahead], axis=1)
    wanted = lax.dynamic_slice_in_dim(mine, 1 - core, 1 + AHEAD, axis=1)
    theirs = lax.ppermute(wanted, "grid", swap)

    first_index = lax.axis_index(("orb", "grid"))
    chosen = jnp.remainder(partners - first_index, total_orbitals).reshape(-1)
    partial = step_without_force(
        planes, before, after, previous.reshape(planes.shape), potential.reshape(planes.shape)
    )
    chosen, partial = lax.optimization_barrier((chosen, partial))
    kept, passed = pair_forces(chosen, offsets[0], mine, theirs)

    received = lax.ppermute(passed, "grid", swap)
    summed = kept + lax.dynamic_update_slice_in_dim(
        jnp.zeros_like(kept), received, 1 - core, axis=1
    )
    returned = exchange(summed).reshape((chips, steps + 1, CORES) + tail)
    folded = sum(
        jnp.pad(returned[:, s], ((s, steps - s),) + ((0, 0),) * (len(tail) + 1))
        for s in range(steps + 1)
    ).reshape(((chips + steps) * CORES,) + tail)
    spilled = from_behind(folded[group:], "orb", 1)
    force = folded[:group] + jnp.pad(spilled, ((0, group - AHEAD),) + ((0, 0),) * len(tail))

    advanced = partial + verlet_factor * force
    return advanced.reshape(orbitals.shape), force.reshape(orbitals.shape)


def solution(mesh):
    in_specs = (
        P("orb", "grid", None),
        P("orb", "grid", None),
        P("orb", "grid", None),
        P(("orb", "grid"), None),
        P(("orb", "grid"), None, None),
    )
    out_specs = (P("orb", "grid", None), P("orb", "grid", None))
    return jax.shard_map(local, mesh=mesh, in_specs=in_specs, out_specs=out_specs, check_vma=False)
```

```python
import functools
import math

import jax
import jax.numpy as jnp
from jax import lax
from jax.experimental import pallas as pl
from jax.experimental.pallas import tpu as pltpu
from jax.sharding import PartitionSpec as P

B = 64
SWEEPS = 4
AHEAD = 4
SHIFT = 16
RELAY_ITEMS = 32
MESH = pl.DeviceIdType.MESH
CORES = 2
LANES = 2 * B
PLANE_ROWS = B // 2
CHUNK = 16
ROW_PAD = SHIFT // 2
PADDED_ROWS = PLANE_ROWS + 3 * ROW_PAD

coulomb_factor = 4.0 * math.pi
exact_share = 0.25
verlet_factor = 0.05
lower_edge = 0.5
upper_edge = 16.0


def sweep_weights():
    centre = 0.5 * (upper_edge + lower_edge)
    radius = 0.5 * (upper_edge - lower_edge)
    ratio_sigma = centre / radius
    previous_rho = 1.0 / ratio_sigma
    weights = []
    for turn_index in range(SWEEPS - 1):
        current_rho = 1.0 / (2.0 * ratio_sigma - previous_rho)
        weights.append((current_rho * previous_rho, 2.0 * current_rho / radius))
        previous_rho = current_rho
    return (centre, weights)


def two_parts(x):
    high = x.astype(jnp.bfloat16)
    low = (x - high.astype(jnp.float32)).astype(jnp.bfloat16)
    return [high, low]


def stencil_matrix():
    source = lax.broadcasted_iota(jnp.int32, (2 * LANES, 2 * LANES), 0) % LANES
    column = lax.broadcasted_iota(jnp.int32, (2 * LANES, 2 * LANES), 1)
    target = column % LANES
    gap = jnp.abs(source - target)
    same = (source // B) == (target // B)
    inside = jnp.where(
        same,
        jnp.where(gap == 0, 90.0, jnp.where(gap == 1, -16.0, jnp.where(gap == 2, 1.0, 0.0))),
        jnp.where(gap == B, -16.0, 0.0),
    )
    across = jnp.where(gap == B, -16.0, 0.0)
    return jnp.where(column < LANES, inside, across).astype(jnp.bfloat16)


def operator12(window, matrix, count):
    rows = count * PLANE_ROWS

    def planes(start):
        return window[start : start + count].reshape(rows, LANES)

    x = planes(2)
    product = jnp.dot(
        jnp.concatenate(two_parts(x), axis=1), matrix, preferred_element_type=jnp.float32
    )
    inside, across = product[:, :LANES], product[:, LANES:]
    lane = lax.broadcasted_iota(jnp.int32, (rows, LANES), 1)
    row = lax.broadcasted_iota(jnp.int32, (rows, LANES), 0) % PLANE_ROWS
    downward = x + jnp.where(lane < B, across, 0.0)
    upward = x + jnp.where(lane >= B, across, 0.0)
    downward = jnp.where(row == 0, 0.0, pltpu.roll(downward, 1, 0))
    upward = jnp.where(row == PLANE_ROWS - 1, 0.0, pltpu.roll(upward, rows - 1, 0))
    beside = planes(0) + planes(4) - 16.0 * (planes(1) + planes(3))
    return inside + downward + upward + beside


def shift_matrix(odd, across):
    shape = (LANES, LANES)
    source = lax.broadcasted_iota(jnp.int32, shape, 0)
    target = lax.broadcasted_iota(jnp.int32, shape, 1)
    cells = (source % B) == (target % B) + across
    half = target // B + odd - source // B

    def one(wanted):
        return jnp.where(cells & (half == wanted), 1.0, 0.0).astype(jnp.bfloat16)

    here, following = one(0), one(2)
    return jnp.concatenate([here, here, following, following], axis=0)


def shifted(padded, first, offset, matrix):
    plane = SHIFT + first + offset[0]
    row = ROW_PAD + (offset[1] >> 1)
    rows = CHUNK * PLANE_ROWS
    here = padded[pl.ds(plane, CHUNK), pl.ds(row, PLANE_ROWS), :].reshape(rows, LANES)
    following = padded[pl.ds(plane, CHUNK), pl.ds(row + 1, PLANE_ROWS), :].reshape(rows, LANES)
    parts = jnp.concatenate(two_parts(here) + two_parts(following), axis=1)
    return jnp.dot(parts, matrix, preferred_element_type=jnp.float32)


def pair_kernel(
    chosen, offsets, mine, theirs, kept, passed,
    padded, own, moved, first, second, residual, total, own_force, stencil, mover,
):
    chips, _, depth = mine.shape[:3]
    core = lax.rem(lax.axis_index("grid"), CORES)
    base = core
    if mine.shape[1] > theirs.shape[1]:
        base = lax.axis_index("grid")
    chunks = B // CHUNK
    centre, weights = sweep_weights()
    shape3 = (CHUNK, PLANE_ROWS, LANES)

    stencil[...] = stencil_matrix()
    zero_plane = jnp.zeros((2, PLANE_ROWS, LANES), jnp.float32)
    for buffer in (first, second):
        buffer[0:2] = zero_plane
        buffer[B + 2 : B + 4] = zero_plane
    own_force[...] = jnp.zeros_like(own_force)
    kept[...] = jnp.zeros_like(kept)
    passed[...] = jnp.zeros_like(passed)

    @pl.loop(0, padded.shape[0])
    def _(plane):
        padded[plane] = jnp.zeros(padded.shape[1:], jnp.float32)

    def slab_start(chip, which):
        return (chip * CORES + which) * depth

    @pl.loop(0, chips)
    def _(chip):
        own[pl.ds(slab_start(chip, core), depth)] = mine[chip, base]
        own[pl.ds(slab_start(chip, 1 - core), depth)] = theirs[chip, core]

    @pl.loop(0, chosen.shape[0])
    def _(pair):
        partner = chosen[pair]
        offset = [offsets[pair, axis] for axis in range(3)]
        inside_rows = pl.ds(ROW_PAD, PLANE_ROWS)

        @pl.loop(0, chips)
        def _(chip):
            padded[pl.ds(SHIFT + slab_start(chip, core), depth), inside_rows, :] = mine[
                chip, base + partner
            ]
            padded[pl.ds(SHIFT + slab_start(chip, 1 - core), depth), inside_rows, :] = theirs[
                chip, core + partner
            ]

        mover[...] = shift_matrix(offset[1] & 1, offset[2])

        @pl.loop(0, chunks)
        def _(chunk):
            at = pl.multiple_of(chunk * CHUNK, CHUNK)
            there = shifted(padded, at, offset, mover[...]).reshape(shape3)
            moved[pl.ds(at, CHUNK)] = there
            start = coulomb_factor * (own[pl.ds(at, CHUNK)] * there)
            residual[pl.ds(at, CHUNK)] = start
            direction = start * (1.0 / centre)
            first[pl.ds(at + 2, CHUNK)] = direction
            total[pl.ds(at, CHUNK)] = direction

        source, target = first, second
        for turn in range(SWEEPS - 1):
            keep_weight, residual_weight = weights[turn]
            last = turn == SWEEPS - 2

            @pl.loop(0, chunks)
            def _(chunk, source=source, target=target, keep=keep_weight, gain=residual_weight, last=last):
                at = pl.multiple_of(chunk * CHUNK, CHUNK)
                window = source[pl.ds(at, CHUNK + 4)]
                applied = operator12(window, stencil[...], CHUNK).reshape(shape3)
                left = residual[pl.ds(at, CHUNK)] - (1.0 / 12.0) * applied
                direction = keep * window[2 : CHUNK + 2] + gain * left
                solved = total[pl.ds(at, CHUNK)] + direction
                if last:
                    own_force[pl.ds(at, CHUNK)] += solved * moved[pl.ds(at, CHUNK)]
                    padded[pl.ds(SHIFT + at, CHUNK), inside_rows, :] = solved * own[pl.ds(at, CHUNK)]
                else:
                    residual[pl.ds(at, CHUNK)] = left
                    target[pl.ds(at + 2, CHUNK)] = direction
                    total[pl.ds(at, CHUNK)] = solved

            source, target = target, source

        back = [-part for part in offset]
        mover[...] = shift_matrix(back[1] & 1, back[2])

        @pl.loop(0, chunks)
        def _(chunk):
            at = pl.multiple_of(chunk * CHUNK, CHUNK)
            there = shifted(padded, at, back, mover[...]).reshape(shape3)
            total[pl.ds(at, CHUNK)] = exact_share * there

        @pl.loop(0, chips)
        def _(chip):
            kept[chip, core + partner] = total[pl.ds(slab_start(chip, core), depth)]
            passed[chip, core + partner] = total[pl.ds(slab_start(chip, 1 - core), depth)]

    @pl.loop(0, chips)
    def _(chip):
        kept[chip, core] = exact_share * own_force[pl.ds(slab_start(chip, core), depth)]
        passed[chip, core] = exact_share * own_force[pl.ds(slab_start(chip, 1 - core), depth)]


def pair_forces(chosen, offsets, mine, theirs):
    box = (B, PLANE_ROWS, LANES)
    f32 = jnp.float32
    vmem = pl.BlockSpec(memory_space=pltpu.VMEM)
    smem = pl.BlockSpec(memory_space=pltpu.SMEM)
    return pl.pallas_call(
        pair_kernel,
        out_shape=(
            jax.ShapeDtypeStruct(theirs.shape, f32),
            jax.ShapeDtypeStruct(theirs.shape, f32),
        ),
        in_specs=[smem, smem, vmem, vmem],
        out_specs=(vmem, vmem),
        scratch_shapes=[
            pltpu.VMEM((B + 2 * SHIFT, PADDED_ROWS, LANES), f32),
            pltpu.VMEM(box, f32),
            pltpu.VMEM(box, f32),
            pltpu.VMEM((B + 4, PLANE_ROWS, LANES), f32),
            pltpu.VMEM((B + 4, PLANE_ROWS, LANES), f32),
            pltpu.VMEM(box, f32),
            pltpu.VMEM(box, f32),
            pltpu.VMEM(box, f32),
            pltpu.VMEM((2 * LANES, 2 * LANES), jnp.bfloat16),
            pltpu.VMEM((4 * LANES, LANES), jnp.bfloat16),
        ],
        compiler_params=pltpu.CompilerParams(vmem_limit_bytes=60 << 20),
        name="pair_forces",
    )(chosen, offsets, mine, theirs)


def step_kernel(now, before, after, previous, potential, partial):
    depth = now.shape[1]
    window = jnp.concatenate([before[0], now[0], after[0]], axis=0)
    applied = operator12(window, stencil_matrix(), depth)
    kinetic = (-0.5 / 12.0) * applied.reshape(now.shape[1:])
    field = now[0]
    partial[0] = (
        2.0 * field - previous[0] + verlet_factor * (kinetic - potential[0] * field)
    )


def step_without_force(now, before, after, previous, potential):
    count = now.shape[0]

    def spec(array):
        return pl.BlockSpec((1,) + array.shape[1:], lambda n: (n, 0, 0, 0))

    operands = (now, before, after, previous, potential)
    return pl.pallas_call(
        step_kernel,
        grid=(count,),
        out_shape=jax.ShapeDtypeStruct(now.shape, jnp.float32),
        in_specs=[spec(array) for array in operands],
        out_specs=spec(now),
        cost_estimate=pl.CostEstimate(
            flops=40 * now.size, bytes_accessed=20 * now.size, transcendentals=0
        ),
        name="step_without_force",
    )(*operands)


def position():
    orb, grid = lax.axis_index("orb"), lax.axis_index("grid")
    return orb, grid, grid // CORES, lax.rem(grid, CORES)


def greet(devices):
    barrier = pltpu.get_barrier_semaphore()
    for there, device in devices:

        @pl.when(there)
        def _(device=device):
            pl.semaphore_signal(barrier, inc=1, device_id=device, device_id_type=MESH)

    pl.semaphore_wait(barrier, sum(there.astype(jnp.int32) for there, _ in devices))


def gather_kernel(
    planes, held, other, local_sem, up_send, right_send, left_send, recv, swap_send, swap_recv
):
    chips, items = held.shape[:2]
    steps = items - chips
    orb, grid, chip, core = position()
    orbs = lax.axis_size("orb")
    sibling = (orb, grid + 1 - 2 * core)
    right, left = (orb, grid + CORES), (orb, grid - CORES)
    up, down = (lax.rem(orb + 1, orbs), grid), (lax.rem(orb + orbs - 1, orbs), grid)
    has_right, has_left, always = chip < chips - 1, chip > 0, chip >= 0
    greet([(always, sibling), (has_right, right), (has_left, left), (always, up), (always, down)])

    def remote(source, target, sent, landed, device):
        return pltpu.make_async_remote_copy(
            src_ref=source, dst_ref=target, send_sem=sent, recv_sem=landed,
            device_id=device, device_id_type=MESH,
        )

    def upward(j):
        k = chips + j
        return remote(planes.at[j], held.at[chip, k], up_send.at[j], recv.at[chip, k], down)

    def rightward(s, k, source):
        return remote(source, held.at[s, k], right_send.at[s, k], recv.at[s, k], right)

    def leftward(s, k, source):
        return remote(source, held.at[s, k], left_send.at[s, k], recv.at[s, k], left)

    def across(s, j, source):
        return remote(source, other.at[s, j], swap_send.at[s, j], swap_recv.at[s, j], sibling)

    def goes_right(k):
        return has_right & (k >= chip + 1)

    def goes_left(k):
        return has_left & (k <= chip - 1 + steps)

    def wanted(k):
        return (k >= chip) & (k <= chip + steps)

    for j in range(steps):
        upward(j).start()
    keep = pltpu.make_async_copy(planes, held.at[chip, pl.ds(0, chips)], local_sem)
    keep.start()

    for first, last, own in ((0, chips, True), (chips, items, False)):

        @pl.loop(first, last)
        def _(k, own=own):
            source = planes.at[k] if own else held.at[chip, k]
            if not own:
                upward(k - chips).wait_recv()

            @pl.when(goes_right(k))
            def _():
                rightward(chip, k, source).start()

            @pl.when(goes_left(k))
            def _():
                leftward(chip, k, source).start()

            @pl.when(wanted(k))
            def _():
                across(chip, k - chip, source).start()

        for hop in range(1, chips):

            @pl.loop(first, last)
            def _(k, hop=hop):
                s = chip - hop

                @pl.when((chip >= hop) & (k >= chip))
                def _():
                    item = held.at[s, k]
                    rightward(s, k, item).wait_recv()

                    @pl.when(goes_right(k))
                    def _():
                        rightward(s, k, item).start()

                    @pl.when(wanted(k))
                    def _():
                        across(s, k - chip, item).start()

                t = chip + hop

                @pl.when((t < chips) & (k <= chip + steps))
                def _():
                    item = held.at[t, k]
                    leftward(t, k, item).wait_recv()

                    @pl.when(goes_left(k))
                    def _():
                        leftward(t, k, item).start()

                    @pl.when(wanted(k))
                    def _():
                        across(t, k - chip, item).start()

    keep.wait()
    for j in range(steps):
        upward(j).wait_send()

    @pl.loop(0, chips)
    def _(s):
        @pl.loop(0, items)
        def _(k):
            item = planes.at[0]

            @pl.when(goes_right(k) & (s <= chip))
            def _():
                rightward(s, k, item).wait_send()

            @pl.when(goes_left(k) & (s >= chip))
            def _():
                leftward(s, k, item).wait_send()

        @pl.loop(0, steps + 1)
        def _(j):
            across(s, j, planes.at[0]).wait()


def gather_boxes(planes, steps):
    chips = planes.shape[0]
    items = chips + steps
    tail = planes.shape[1:]
    anywhere = pl.BlockSpec(memory_space=pl.ANY)
    dma = pltpu.SemaphoreType.DMA
    return pl.pallas_call(
        gather_kernel,
        out_shape=(
            jax.ShapeDtypeStruct((chips, items) + tail, planes.dtype),
            jax.ShapeDtypeStruct((chips, steps + 1) + tail, planes.dtype),
        ),
        in_specs=[pl.BlockSpec(memory_space=pltpu.VMEM)],
        out_specs=(anywhere, anywhere),
        scratch_shapes=[
            dma, dma((steps,)), dma((chips, items)), dma((chips, items)), dma((chips, items)),
            dma((chips, steps + 1)), dma((chips, steps + 1)),
        ],
        compiler_params=pltpu.CompilerParams(
            collective_id=0, has_side_effects=True, vmem_limit_bytes=8 << 20
        ),
        name="gather_boxes",
    )(planes)


def return_kernel(
    kept, passed, folded, sibling_in, left_in, right_in,
    swap_send, swap_recv, left_send, left_recv, right_send, right_recv,
):
    chips, items = left_in.shape[:2]
    steps = items - chips
    orb, grid, chip, core = position()
    sibling = (orb, grid + 1 - 2 * core)
    right, left = (orb, grid + CORES), (orb, grid - CORES)
    has_right, has_left, always = chip < chips - 1, chip > 0, chip >= 0
    greet([(always, sibling), (has_right, right), (has_left, left)])

    def remote(source, target, sent, landed, device):
        return pltpu.make_async_remote_copy(
            src_ref=source, dst_ref=target, send_sem=sent, recv_sem=landed,
            device_id=device, device_id_type=MESH,
        )

    def across(s, j):
        return remote(
            passed.at[s, j], sibling_in.at[s, j], swap_send.at[s, j], swap_recv.at[s, j], sibling
        )

    def leftward(s, k):
        return remote(
            left_in.at[s, k], left_in.at[s, k], left_send.at[s, k], left_recv.at[s, k], left
        )

    def rightward(s, k):
        return remote(
            right_in.at[s, k], right_in.at[s, k], right_send.at[s, k], right_recv.at[s, k], right
        )

    def from_right(k):
        return has_right & (k >= chip + 1)

    def from_left(k):
        return has_left & (k <= chip - 1 + steps)

    def contributes(k):
        return (k >= chip) & (k <= chip + steps)

    def share(s, k):
        return kept[s, k - chip] + sibling_in[s, k - chip]

    for turn in range(chips):
        for s, leaves in ((turn, chip > turn), (chips - 1 - turn, chip < chips - 1 - turn)):

            @pl.loop(0, steps + 1)
            def _(j, s=s, leaves=leaves):
                @pl.when(leaves)
                def _():
                    across(s, j).start()

    @pl.loop(0, steps + 1)
    def _(j):
        across(chip, j).start()

    for turn in range(chips - 1):

        @pl.loop(0, items)
        def _(k, s=turn):
            @pl.when((s < chip) & (k >= chip))
            def _():
                @pl.when(contributes(k))
                def _():
                    across(s, k - chip).wait_recv()

                @pl.when(from_right(k))
                def _():
                    leftward(s, k).wait_recv()

                    @pl.when(contributes(k))
                    def _():
                        left_in[s, k] += share(s, k)

                @pl.when(jnp.logical_not(from_right(k)))
                def _():
                    left_in[s, k] = share(s, k)

                leftward(s, k).start()

        @pl.loop(0, items)
        def _(k, s=chips - 1 - turn):
            @pl.when((s > chip) & (k <= chip + steps))
            def _():
                @pl.when(contributes(k))
                def _():
                    across(s, k - chip).wait_recv()

                @pl.when(from_left(k))
                def _():
                    rightward(s, k).wait_recv()

                    @pl.when(contributes(k))
                    def _():
                        right_in[s, k] += share(s, k)

                @pl.when(jnp.logical_not(from_left(k)))
                def _():
                    right_in[s, k] = share(s, k)

                rightward(s, k).start()

    @pl.loop(0, items)
    def _(k):
        folded[k] = jnp.zeros(folded.shape[1:], folded.dtype)

        @pl.when(contributes(k))
        def _():
            across(chip, k - chip).wait_recv()
            folded[k] = share(chip, k)

        @pl.when(from_right(k))
        def _():
            leftward(chip, k).wait_recv()
            folded[k] += left_in[chip, k]

        @pl.when(from_left(k))
        def _():
            rightward(chip, k).wait_recv()
            folded[k] += right_in[chip, k]

    @pl.loop(0, chips)
    def _(s):
        @pl.loop(0, steps + 1)
        def _(j):
            across(s, j).wait_send()

        @pl.loop(0, items)
        def _(k):
            @pl.when((s < chip) & (k >= chip))
            def _():
                leftward(s, k).wait_send()

            @pl.when((s > chip) & (k <= chip + steps))
            def _():
                rightward(s, k).wait_send()


def return_forces(kept, passed):
    chips, span = kept.shape[:2]
    items = chips + span - 1
    tail = kept.shape[2:]
    vmem = pl.BlockSpec(memory_space=pltpu.VMEM)
    dma = pltpu.SemaphoreType.DMA
    line = (chips, items)
    return pl.pallas_call(
        return_kernel,
        out_shape=jax.ShapeDtypeStruct((items,) + tail, kept.dtype),
        in_specs=[vmem, vmem],
        out_specs=vmem,
        scratch_shapes=[
            pltpu.VMEM(kept.shape, kept.dtype),
            pltpu.VMEM(line + tail, kept.dtype),
            pltpu.VMEM(line + tail, kept.dtype),
            dma((chips, span)), dma((chips, span)), dma(line), dma(line), dma(line), dma(line),
        ],
        compiler_params=pltpu.CompilerParams(
            collective_id=1, has_side_effects=True, vmem_limit_bytes=40 << 20
        ),
        name="return_forces",
    )(kept, passed)


def from_behind(array, axis, by):
    count = lax.axis_size(axis)
    return lax.ppermute(array, axis, [(i, (i + by) % count) for i in range(count)])


def neighbour_planes(planes):
    count = lax.axis_size("grid")
    depth = planes.shape[1]
    before, after = [], []
    for hop in range(1, -(-2 // depth) + 1):
        size = min(depth, 2 - (hop - 1) * depth)
        forward = [(i, i + hop) for i in range(count - hop)]
        backward = [(i + hop, i) for i in range(count - hop)]
        before.insert(0, lax.ppermute(planes[:, depth - size :], "grid", forward))
        after.append(lax.ppermute(planes[:, :size], "grid", backward))
    return jnp.concatenate(before, axis=1), jnp.concatenate(after, axis=1)


def local(orbitals, previous, potential, partners, offsets):
    slabs = lax.axis_size("grid")
    chips = slabs // CORES
    total_orbitals = lax.axis_size(("orb", "grid"))
    group, rows, width = orbitals.shape
    depth = rows // PLANE_ROWS
    planes = orbitals.reshape(group, depth, PLANE_ROWS, width)
    tail = planes.shape[1:]
    steps = AHEAD // CORES
    across = [[chip * CORES + c for chip in range(chips)] for c in range(CORES)]
    swap = [(i, i + 1 - 2 * (i % CORES)) for i in range(slabs)]

    before, after = neighbour_planes(planes)
    by_chip = (chips, CORES) + tail
    boxes = (CORES * (steps + 1),) + tail
    relayed = chips * (chips + steps) <= RELAY_ITEMS

    def exchange(array):
        return lax.all_to_all(
            array, "grid", split_axis=0, concat_axis=0, axis_index_groups=across, tiled=True
        )

    if relayed:
        mine, theirs = gather_boxes(planes.reshape(by_chip), steps)
        mine = mine.reshape((chips, CORES * (chips + steps)) + tail)
        theirs = theirs.reshape((chips,) + boxes)
    else:
        upper = from_behind(planes[:AHEAD], "orb", -1)
        blocks = jnp.concatenate([planes, upper], axis=0).reshape((chips + steps, CORES) + tail)
        own_group = exchange(planes.reshape(by_chip))
        ahead = exchange(
            jnp.concatenate([blocks[s : s + chips] for s in range(1, steps + 1)], axis=1)
        )
        mine = jnp.concatenate([own_group, ahead], axis=1)
        theirs = lax.ppermute(mine, "grid", swap)

    first_index = lax.axis_index(("orb", "grid"))
    chosen = jnp.remainder(partners - first_index, total_orbitals).reshape(-1)
    partial = step_without_force(
        planes, before, after, previous.reshape(planes.shape), potential.reshape(planes.shape)
    )
    chosen, partial = lax.optimization_barrier((chosen, partial))
    kept, passed = pair_forces(chosen, offsets[0], mine, theirs)

    if relayed:
        pairs = (chips, steps + 1, CORES) + tail
        folded = return_forces(kept.reshape(pairs), passed.reshape(pairs))
    else:
        summed = kept + lax.ppermute(passed, "grid", swap)
        returned = exchange(summed).reshape((chips, steps + 1, CORES) + tail)
        folded = sum(
            jnp.pad(returned[:, s], ((s, steps - s),) + ((0, 0),) * (len(tail) + 1))
            for s in range(steps + 1)
        )
    folded = folded.reshape(((chips + steps) * CORES,) + tail)
    spilled = from_behind(folded[group:], "orb", 1)
    force = folded[:group] + jnp.pad(spilled, ((0, group - AHEAD),) + ((0, 0),) * len(tail))

    advanced = partial + verlet_factor * force
    return advanced.reshape(orbitals.shape), force.reshape(orbitals.shape)


def solution(mesh):
    in_specs = (
        P("orb", "grid", None),
        P("orb", "grid", None),
        P("orb", "grid", None),
        P(("orb", "grid"), None),
        P(("orb", "grid"), None, None),
    )
    out_specs = (P("orb", "grid", None), P("orb", "grid", None))
    return jax.shard_map(local, mesh=mesh, in_specs=in_specs, out_specs=out_specs, check_vma=False)
```

```python
import functools
import math

import jax
import jax.numpy as jnp
from jax import lax
from jax.experimental import pallas as pl
from jax.experimental.pallas import tpu as pltpu
from jax.sharding import PartitionSpec as P

B = 64
SWEEPS = 4
AHEAD = 4
SHIFT = 16
RELAY_ITEMS = 32
MESH = pl.DeviceIdType.MESH
CORES = 2
LANES = 2 * B
PLANE_ROWS = B // 2
CHUNK = 16
ROW_PAD = SHIFT // 2
PADDED_ROWS = PLANE_ROWS + 3 * ROW_PAD

coulomb_factor = 4.0 * math.pi
exact_share = 0.25
verlet_factor = 0.05
lower_edge = 0.5
upper_edge = 16.0


def sweep_weights():
    centre = 0.5 * (upper_edge + lower_edge)
    radius = 0.5 * (upper_edge - lower_edge)
    ratio_sigma = centre / radius
    previous_rho = 1.0 / ratio_sigma
    weights = []
    for turn_index in range(SWEEPS - 1):
        current_rho = 1.0 / (2.0 * ratio_sigma - previous_rho)
        weights.append((current_rho * previous_rho, 2.0 * current_rho / radius))
        previous_rho = current_rho
    return (centre, weights)


def two_parts(x):
    high = x.astype(jnp.bfloat16)
    low = (x - high.astype(jnp.float32)).astype(jnp.bfloat16)
    return [high, low]


def stencil_matrix():
    source = lax.broadcasted_iota(jnp.int32, (2 * LANES, 2 * LANES), 0) % LANES
    column = lax.broadcasted_iota(jnp.int32, (2 * LANES, 2 * LANES), 1)
    target = column % LANES
    gap = jnp.abs(source - target)
    same = (source // B) == (target // B)
    inside = jnp.where(
        same,
        jnp.where(gap == 0, 90.0, jnp.where(gap == 1, -16.0, jnp.where(gap == 2, 1.0, 0.0))),
        jnp.where(gap == B, -16.0, 0.0),
    )
    across = jnp.where(gap == B, -16.0, 0.0)
    return jnp.where(column < LANES, inside, across).astype(jnp.bfloat16)


def operator12(window, matrix, count):
    rows = count * PLANE_ROWS

    def planes(start):
        return window[start : start + count].reshape(rows, LANES)

    x = planes(2)
    product = jnp.dot(
        jnp.concatenate(two_parts(x), axis=1), matrix, preferred_element_type=jnp.float32
    )
    inside, across = product[:, :LANES], product[:, LANES:]
    lane = lax.broadcasted_iota(jnp.int32, (rows, LANES), 1)
    row = lax.broadcasted_iota(jnp.int32, (rows, LANES), 0) % PLANE_ROWS
    downward = x + jnp.where(lane < B, across, 0.0)
    upward = x + jnp.where(lane >= B, across, 0.0)
    downward = jnp.where(row == 0, 0.0, pltpu.roll(downward, 1, 0))
    upward = jnp.where(row == PLANE_ROWS - 1, 0.0, pltpu.roll(upward, rows - 1, 0))
    beside = planes(0) + planes(4) - 16.0 * (planes(1) + planes(3))
    return inside + downward + upward + beside


def shift_matrix(odd, across):
    shape = (LANES, LANES)
    source = lax.broadcasted_iota(jnp.int32, shape, 0)
    target = lax.broadcasted_iota(jnp.int32, shape, 1)
    cells = (source % B) == (target % B) + across
    half = target // B + odd - source // B

    def one(wanted):
        return jnp.where(cells & (half == wanted), 1.0, 0.0).astype(jnp.bfloat16)

    here, following = one(0), one(2)
    return jnp.concatenate([here, here, following, following], axis=0)


def shifted(padded, first, offset, matrix):
    plane = SHIFT + first + offset[0]
    row = ROW_PAD + (offset[1] >> 1)
    rows = CHUNK * PLANE_ROWS
    here = padded[pl.ds(plane, CHUNK), pl.ds(row, PLANE_ROWS), :].reshape(rows, LANES)
    following = padded[pl.ds(plane, CHUNK), pl.ds(row + 1, PLANE_ROWS), :].reshape(rows, LANES)
    parts = jnp.concatenate(two_parts(here) + two_parts(following), axis=1)
    return jnp.dot(parts, matrix, preferred_element_type=jnp.float32)


def pair_kernel(
    chosen, offsets, mine, theirs, kept, passed,
    padded, own, moved, first, second, residual, total, own_force, stencil, mover,
):
    chips, _, depth = mine.shape[:3]
    core = lax.rem(lax.axis_index("grid"), CORES)
    base = core
    if mine.shape[1] > theirs.shape[1]:
        base = lax.axis_index("grid")
    chunks = B // CHUNK
    centre, weights = sweep_weights()
    shape3 = (CHUNK, PLANE_ROWS, LANES)

    stencil[...] = stencil_matrix()
    zero_plane = jnp.zeros((2, PLANE_ROWS, LANES), jnp.float32)
    for buffer in (first, second):
        buffer[0:2] = zero_plane
        buffer[B + 2 : B + 4] = zero_plane
    own_force[...] = jnp.zeros_like(own_force)
    kept[...] = jnp.zeros_like(kept)
    passed[...] = jnp.zeros_like(passed)

    @pl.loop(0, padded.shape[0])
    def _(plane):
        padded[plane] = jnp.zeros(padded.shape[1:], jnp.float32)

    def slab_start(chip, which):
        return (chip * CORES + which) * depth

    @pl.loop(0, chips)
    def _(chip):
        own[pl.ds(slab_start(chip, core), depth)] = mine[chip, base]
        own[pl.ds(slab_start(chip, 1 - core), depth)] = theirs[chip, core]

    @pl.loop(0, chosen.shape[0])
    def _(pair):
        partner = chosen[pair]
        offset = [offsets[pair, axis] for axis in range(3)]
        inside_rows = pl.ds(ROW_PAD, PLANE_ROWS)

        @pl.loop(0, chips)
        def _(chip):
            padded[pl.ds(SHIFT + slab_start(chip, core), depth), inside_rows, :] = mine[
                chip, base + partner
            ]
            padded[pl.ds(SHIFT + slab_start(chip, 1 - core), depth), inside_rows, :] = theirs[
                chip, core + partner
            ]

        mover[...] = shift_matrix(offset[1] & 1, offset[2])

        @pl.loop(0, chunks)
        def _(chunk):
            at = pl.multiple_of(chunk * CHUNK, CHUNK)
            there = shifted(padded, at, offset, mover[...]).reshape(shape3)
            moved[pl.ds(at, CHUNK)] = there
            start = coulomb_factor * (own[pl.ds(at, CHUNK)] * there)
            residual[pl.ds(at, CHUNK)] = start
            direction = start * (1.0 / centre)
            first[pl.ds(at + 2, CHUNK)] = direction
            total[pl.ds(at, CHUNK)] = direction

        source, target = first, second
        for turn in range(SWEEPS - 1):
            keep_weight, residual_weight = weights[turn]
            last = turn == SWEEPS - 2

            @pl.loop(0, chunks)
            def _(chunk, source=source, target=target, keep=keep_weight, gain=residual_weight, last=last):
                at = pl.multiple_of(chunk * CHUNK, CHUNK)
                window = source[pl.ds(at, CHUNK + 4)]
                applied = operator12(window, stencil[...], CHUNK).reshape(shape3)
                left = residual[pl.ds(at, CHUNK)] - (1.0 / 12.0) * applied
                direction = keep * window[2 : CHUNK + 2] + gain * left
                solved = total[pl.ds(at, CHUNK)] + direction
                if last:
                    own_force[pl.ds(at, CHUNK)] += solved * moved[pl.ds(at, CHUNK)]
                    padded[pl.ds(SHIFT + at, CHUNK), inside_rows, :] = solved * own[pl.ds(at, CHUNK)]
                else:
                    residual[pl.ds(at, CHUNK)] = left
                    target[pl.ds(at + 2, CHUNK)] = direction
                    total[pl.ds(at, CHUNK)] = solved

            source, target = target, source

        back = [-part for part in offset]
        mover[...] = shift_matrix(back[1] & 1, back[2])

        @pl.loop(0, chunks)
        def _(chunk):
            at = pl.multiple_of(chunk * CHUNK, CHUNK)
            there = shifted(padded, at, back, mover[...]).reshape(shape3)
            total[pl.ds(at, CHUNK)] = exact_share * there

        @pl.loop(0, chips)
        def _(chip):
            kept[chip, core + partner] = total[pl.ds(slab_start(chip, core), depth)]
            passed[chip, core + partner] = total[pl.ds(slab_start(chip, 1 - core), depth)]

    @pl.loop(0, chips)
    def _(chip):
        kept[chip, core] = exact_share * own_force[pl.ds(slab_start(chip, core), depth)]
        passed[chip, core] = exact_share * own_force[pl.ds(slab_start(chip, 1 - core), depth)]


def pair_forces(chosen, offsets, mine, theirs):
    box = (B, PLANE_ROWS, LANES)
    f32 = jnp.float32
    vmem = pl.BlockSpec(memory_space=pltpu.VMEM)
    smem = pl.BlockSpec(memory_space=pltpu.SMEM)
    return pl.pallas_call(
        pair_kernel,
        out_shape=(
            jax.ShapeDtypeStruct(theirs.shape, f32),
            jax.ShapeDtypeStruct(theirs.shape, f32),
        ),
        in_specs=[smem, smem, vmem, vmem],
        out_specs=(vmem, vmem),
        scratch_shapes=[
            pltpu.VMEM((B + 2 * SHIFT, PADDED_ROWS, LANES), f32),
            pltpu.VMEM(box, f32),
            pltpu.VMEM(box, f32),
            pltpu.VMEM((B + 4, PLANE_ROWS, LANES), f32),
            pltpu.VMEM((B + 4, PLANE_ROWS, LANES), f32),
            pltpu.VMEM(box, f32),
            pltpu.VMEM(box, f32),
            pltpu.VMEM(box, f32),
            pltpu.VMEM((2 * LANES, 2 * LANES), jnp.bfloat16),
            pltpu.VMEM((4 * LANES, LANES), jnp.bfloat16),
        ],
        compiler_params=pltpu.CompilerParams(vmem_limit_bytes=60 << 20),
        name="pair_forces",
    )(chosen, offsets, mine, theirs)


def step_kernel(now, before, after, previous, potential, partial):
    depth = now.shape[1]
    window = jnp.concatenate([before[0], now[0], after[0]], axis=0)
    applied = operator12(window, stencil_matrix(), depth)
    kinetic = (-0.5 / 12.0) * applied.reshape(now.shape[1:])
    field = now[0]
    partial[0] = (
        2.0 * field - previous[0] + verlet_factor * (kinetic - potential[0] * field)
    )


def step_without_force(now, before, after, previous, potential):
    count = now.shape[0]

    def spec(array):
        return pl.BlockSpec((1,) + array.shape[1:], lambda n: (n, 0, 0, 0))

    operands = (now, before, after, previous, potential)
    return pl.pallas_call(
        step_kernel,
        grid=(count,),
        out_shape=jax.ShapeDtypeStruct(now.shape, jnp.float32),
        in_specs=[spec(array) for array in operands],
        out_specs=spec(now),
        cost_estimate=pl.CostEstimate(
            flops=40 * now.size, bytes_accessed=20 * now.size, transcendentals=0
        ),
        name="step_without_force",
    )(*operands)


LINK_TIME = 5.6
HOP_TIME = 2.0
UPPER_TIME = 12.0


def arrival_orders(chips, steps, gathering):
    items = chips + steps
    pending, orders, free = [], [[] for _ in range(chips)], {}
    for chip in range(chips):
        for flow in (1, -1):
            for s in range(chips):
                for k in range(items):
                    if gathering:
                        starts = s == chip
                        last = min(k, chips - 1) if flow > 0 else max(0, k - steps)
                        hops = (last - chip) * flow
                        ready = 0.0 if k < chips else UPPER_TIME
                    else:
                        hops = (s - chip) * flow
                        alone = k == chip + steps if flow > 0 else k == chip
                        edge = chip == 0 if flow > 0 else chip == chips - 1
                        starts = chip <= k <= chip + steps and (alone or edge)
                        ready = 1.0
                    if starts and hops > 0:
                        pending.append((ready, -hops, chip, flow, s, k, hops))
    while pending:
        pending.sort()
        ready, _, chip, flow, s, k, hops = pending.pop(0)
        orders[chip].append((ready, flow, s, k))
        if hops > 0:
            sent = max(ready, free.get((chip, flow), 0.0)) + LINK_TIME
            free[chip, flow] = sent
            pending.append((sent + HOP_TIME, 1 - hops, chip + flow, flow, s, k, hops - 1))
    return orders


def position():
    orb, grid = lax.axis_index("orb"), lax.axis_index("grid")
    return orb, grid, grid // CORES, lax.rem(grid, CORES)


def greet(devices):
    barrier = pltpu.get_barrier_semaphore()
    for there, device in devices:

        @pl.when(there)
        def _(device=device):
            pl.semaphore_signal(barrier, inc=1, device_id=device, device_id_type=MESH)

    pl.semaphore_wait(barrier, sum(there.astype(jnp.int32) for there, _ in devices))


def gather_kernel(
    planes, held, other, local_sem, up_send, right_send, left_send, recv, swap_send, swap_recv
):
    chips, items = held.shape[:2]
    steps = items - chips
    orb, grid, chip, core = position()
    orbs = lax.axis_size("orb")
    sibling = (orb, grid + 1 - 2 * core)
    right, left = (orb, grid + CORES), (orb, grid - CORES)
    up, down = (lax.rem(orb + 1, orbs), grid), (lax.rem(orb + orbs - 1, orbs), grid)
    has_right, has_left, always = chip < chips - 1, chip > 0, chip >= 0
    greet([(always, sibling), (has_right, right), (has_left, left), (always, up), (always, down)])

    def remote(source, target, sent, landed, device):
        return pltpu.make_async_remote_copy(
            src_ref=source, dst_ref=target, send_sem=sent, recv_sem=landed,
            device_id=device, device_id_type=MESH,
        )

    def upward(j):
        k = chips + j
        return remote(planes.at[j], held.at[chip, k], up_send.at[j], recv.at[chip, k], down)

    def rightward(s, k, source):
        return remote(source, held.at[s, k], right_send.at[s, k], recv.at[s, k], right)

    def leftward(s, k, source):
        return remote(source, held.at[s, k], left_send.at[s, k], recv.at[s, k], left)

    def across(s, j, source):
        return remote(source, other.at[s, j], swap_send.at[s, j], swap_recv.at[s, j], sibling)

    def goes_right(k):
        return has_right & (k >= chip + 1)

    def goes_left(k):
        return has_left & (k <= chip - 1 + steps)

    def wanted(k):
        return (k >= chip) & (k <= chip + steps)

    for j in range(steps):
        upward(j).start()
    keep = pltpu.make_async_copy(planes, held.at[chip, pl.ds(0, chips)], local_sem)
    keep.start()

    for here, order in enumerate(arrival_orders(chips, steps, True)):

        @pl.when(chip == here)
        def _(here=here, order=order):
            arrived, swapped = set(), set()
            for _, flow, slab, k in order:
                own = slab == here
                item = planes.at[k] if own and k < chips else held.at[slab, k]
                send = rightward if flow > 0 else leftward
                if own and k >= chips and k not in arrived:
                    upward(k - chips).wait_recv()
                    arrived.add(k)
                if not own:
                    send(slab, k, item).wait_recv()
                onward = here + 1 <= min(k, chips - 1) if flow > 0 else here - 1 >= max(0, k - steps)
                if onward:
                    send(slab, k, item).start()
                if here <= k <= here + steps and (slab, k) not in swapped:
                    across(slab, k - here, item).start()
                    swapped.add((slab, k))
            for k in range(chips, items):
                if k not in arrived:
                    upward(k - chips).wait_recv()
            for k in range(here, here + steps + 1):
                if (here, k) not in swapped:
                    across(here, k - here, planes.at[k] if k < chips else held.at[here, k]).start()

    keep.wait()
    for j in range(steps):
        upward(j).wait_send()

    @pl.loop(0, chips)
    def _(s):
        @pl.loop(0, items)
        def _(k):
            item = planes.at[0]

            @pl.when(goes_right(k) & (s <= chip))
            def _():
                rightward(s, k, item).wait_send()

            @pl.when(goes_left(k) & (s >= chip))
            def _():
                leftward(s, k, item).wait_send()

        @pl.loop(0, steps + 1)
        def _(j):
            across(s, j, planes.at[0]).wait()


def gather_boxes(planes, steps):
    chips = planes.shape[0]
    items = chips + steps
    tail = planes.shape[1:]
    anywhere = pl.BlockSpec(memory_space=pl.ANY)
    dma = pltpu.SemaphoreType.DMA
    return pl.pallas_call(
        gather_kernel,
        out_shape=(
            jax.ShapeDtypeStruct((chips, items) + tail, planes.dtype),
            jax.ShapeDtypeStruct((chips, steps + 1) + tail, planes.dtype),
        ),
        in_specs=[pl.BlockSpec(memory_space=pltpu.VMEM)],
        out_specs=(anywhere, anywhere),
        scratch_shapes=[
            dma, dma((steps,)), dma((chips, items)), dma((chips, items)), dma((chips, items)),
            dma((chips, steps + 1)), dma((chips, steps + 1)),
        ],
        compiler_params=pltpu.CompilerParams(
            collective_id=0, has_side_effects=True, vmem_limit_bytes=8 << 20
        ),
        name="gather_boxes",
    )(planes)


def return_kernel(
    kept, passed, folded, sibling_in, left_in, right_in,
    swap_send, swap_recv, left_send, left_recv, right_send, right_recv,
):
    chips, items = left_in.shape[:2]
    steps = items - chips
    orb, grid, chip, core = position()
    sibling = (orb, grid + 1 - 2 * core)
    right, left = (orb, grid + CORES), (orb, grid - CORES)
    has_right, has_left, always = chip < chips - 1, chip > 0, chip >= 0
    greet([(always, sibling), (has_right, right), (has_left, left)])

    def remote(source, target, sent, landed, device):
        return pltpu.make_async_remote_copy(
            src_ref=source, dst_ref=target, send_sem=sent, recv_sem=landed,
            device_id=device, device_id_type=MESH,
        )

    def across(s, j):
        return remote(
            passed.at[s, j], sibling_in.at[s, j], swap_send.at[s, j], swap_recv.at[s, j], sibling
        )

    def leftward(s, k):
        return remote(
            left_in.at[s, k], left_in.at[s, k], left_send.at[s, k], left_recv.at[s, k], left
        )

    def rightward(s, k):
        return remote(
            right_in.at[s, k], right_in.at[s, k], right_send.at[s, k], right_recv.at[s, k], right
        )

    def from_right(k):
        return has_right & (k >= chip + 1)

    def from_left(k):
        return has_left & (k <= chip - 1 + steps)

    def contributes(k):
        return (k >= chip) & (k <= chip + steps)

    def share(s, k):
        return kept[s, k - chip] + sibling_in[s, k - chip]

    for turn in range(chips):
        for s, leaves in ((turn, chip > turn), (chips - 1 - turn, chip < chips - 1 - turn)):

            @pl.loop(0, steps + 1)
            def _(j, s=s, leaves=leaves):
                @pl.when(leaves)
                def _():
                    across(s, j).start()

    @pl.loop(0, steps + 1)
    def _(j):
        across(chip, j).start()

    for here, order in enumerate(arrival_orders(chips, steps, False)):

        @pl.when(chip == here)
        def _(here=here, order=order):
            swapped = set()
            for _, flow, slab, k in order:
                if slab == here:
                    continue
                buffer, send = (right_in, rightward) if flow > 0 else (left_in, leftward)
                alone = (here == 0 or k == here + steps) if flow > 0 else (here == chips - 1 or k == here)
                if not alone:
                    send(slab, k).wait_recv()
                if here <= k <= here + steps:
                    if (slab, k) not in swapped:
                        across(slab, k - here).wait_recv()
                        swapped.add((slab, k))
                    added = kept[slab, k - here] + sibling_in[slab, k - here]
                    buffer[slab, k] = added if alone else buffer[slab, k] + added
                send(slab, k).start()

    @pl.loop(0, items)
    def _(k):
        folded[k] = jnp.zeros(folded.shape[1:], folded.dtype)

        @pl.when(contributes(k))
        def _():
            across(chip, k - chip).wait_recv()
            folded[k] = share(chip, k)

        @pl.when(from_right(k))
        def _():
            leftward(chip, k).wait_recv()
            folded[k] += left_in[chip, k]

        @pl.when(from_left(k))
        def _():
            rightward(chip, k).wait_recv()
            folded[k] += right_in[chip, k]

    @pl.loop(0, chips)
    def _(s):
        @pl.loop(0, steps + 1)
        def _(j):
            across(s, j).wait_send()

        @pl.loop(0, items)
        def _(k):
            @pl.when((s < chip) & (k >= chip))
            def _():
                leftward(s, k).wait_send()

            @pl.when((s > chip) & (k <= chip + steps))
            def _():
                rightward(s, k).wait_send()


def return_forces(kept, passed):
    chips, span = kept.shape[:2]
    items = chips + span - 1
    tail = kept.shape[2:]
    vmem = pl.BlockSpec(memory_space=pltpu.VMEM)
    dma = pltpu.SemaphoreType.DMA
    line = (chips, items)
    return pl.pallas_call(
        return_kernel,
        out_shape=jax.ShapeDtypeStruct((items,) + tail, kept.dtype),
        in_specs=[vmem, vmem],
        out_specs=vmem,
        scratch_shapes=[
            pltpu.VMEM(kept.shape, kept.dtype),
            pltpu.VMEM(line + tail, kept.dtype),
            pltpu.VMEM(line + tail, kept.dtype),
            dma((chips, span)), dma((chips, span)), dma(line), dma(line), dma(line), dma(line),
        ],
        compiler_params=pltpu.CompilerParams(
            collective_id=1, has_side_effects=True, vmem_limit_bytes=40 << 20
        ),
        name="return_forces",
    )(kept, passed)


def from_behind(array, axis, by):
    count = lax.axis_size(axis)
    return lax.ppermute(array, axis, [(i, (i + by) % count) for i in range(count)])


def neighbour_planes(planes):
    count = lax.axis_size("grid")
    depth = planes.shape[1]
    before, after = [], []
    for hop in range(1, -(-2 // depth) + 1):
        size = min(depth, 2 - (hop - 1) * depth)
        forward = [(i, i + hop) for i in range(count - hop)]
        backward = [(i + hop, i) for i in range(count - hop)]
        before.insert(0, lax.ppermute(planes[:, depth - size :], "grid", forward))
        after.append(lax.ppermute(planes[:, :size], "grid", backward))
    return jnp.concatenate(before, axis=1), jnp.concatenate(after, axis=1)


def local(orbitals, previous, potential, partners, offsets):
    slabs = lax.axis_size("grid")
    chips = slabs // CORES
    total_orbitals = lax.axis_size(("orb", "grid"))
    group, rows, width = orbitals.shape
    depth = rows // PLANE_ROWS
    planes = orbitals.reshape(group, depth, PLANE_ROWS, width)
    tail = planes.shape[1:]
    steps = AHEAD // CORES
    across = [[chip * CORES + c for chip in range(chips)] for c in range(CORES)]
    swap = [(i, i + 1 - 2 * (i % CORES)) for i in range(slabs)]

    before, after = neighbour_planes(planes)
    by_chip = (chips, CORES) + tail
    boxes = (CORES * (steps + 1),) + tail
    relayed = chips * (chips + steps) <= RELAY_ITEMS

    def exchange(array):
        return lax.all_to_all(
            array, "grid", split_axis=0, concat_axis=0, axis_index_groups=across, tiled=True
        )

    if relayed:
        mine, theirs = gather_boxes(planes.reshape(by_chip), steps)
        mine = mine.reshape((chips, CORES * (chips + steps)) + tail)
        theirs = theirs.reshape((chips,) + boxes)
    else:
        upper = from_behind(planes[:AHEAD], "orb", -1)
        blocks = jnp.concatenate([planes, upper], axis=0).reshape((chips + steps, CORES) + tail)
        own_group = exchange(planes.reshape(by_chip))
        ahead = exchange(
            jnp.concatenate([blocks[s : s + chips] for s in range(1, steps + 1)], axis=1)
        )
        mine = jnp.concatenate([own_group, ahead], axis=1)
        theirs = lax.ppermute(mine, "grid", swap)

    first_index = lax.axis_index(("orb", "grid"))
    chosen = jnp.remainder(partners - first_index, total_orbitals).reshape(-1)
    partial = step_without_force(
        planes, before, after, previous.reshape(planes.shape), potential.reshape(planes.shape)
    )
    chosen, partial = lax.optimization_barrier((chosen, partial))
    kept, passed = pair_forces(chosen, offsets[0], mine, theirs)

    if relayed:
        pairs = (chips, steps + 1, CORES) + tail
        folded = return_forces(kept.reshape(pairs), passed.reshape(pairs))
    else:
        summed = kept + lax.ppermute(passed, "grid", swap)
        returned = exchange(summed).reshape((chips, steps + 1, CORES) + tail)
        folded = sum(
            jnp.pad(returned[:, s], ((s, steps - s),) + ((0, 0),) * (len(tail) + 1))
            for s in range(steps + 1)
        )
    folded = folded.reshape(((chips + steps) * CORES,) + tail)
    spilled = from_behind(folded[group:], "orb", 1)
    force = folded[:group] + jnp.pad(spilled, ((0, group - AHEAD),) + ((0, 0),) * len(tail))

    advanced = partial + verlet_factor * force
    return advanced.reshape(orbitals.shape), force.reshape(orbitals.shape)


def solution(mesh):
    in_specs = (
        P("orb", "grid", None),
        P("orb", "grid", None),
        P("orb", "grid", None),
        P(("orb", "grid"), None),
        P(("orb", "grid"), None, None),
    )
    out_specs = (P("orb", "grid", None), P("orb", "grid", None))
    return jax.shard_map(local, mesh=mesh, in_specs=in_specs, out_specs=out_specs, check_vma=False)
```

```python
import functools
import math

import jax
import jax.numpy as jnp
from jax import lax
from jax.experimental import pallas as pl
from jax.experimental.pallas import tpu as pltpu
from jax.sharding import PartitionSpec as P

B = 64
SWEEPS = 4
AHEAD = 4
SHIFT = 16
RELAY_ITEMS = 32
MESH = pl.DeviceIdType.MESH
CORES = 2
LANES = 2 * B
PLANE_ROWS = B // 2
CHUNK = 32
ROW_PAD = SHIFT // 2
PADDED_ROWS = PLANE_ROWS + 3 * ROW_PAD

coulomb_factor = 4.0 * math.pi
exact_share = 0.25
verlet_factor = 0.05
lower_edge = 0.5
upper_edge = 16.0


def sweep_weights():
    centre = 0.5 * (upper_edge + lower_edge)
    radius = 0.5 * (upper_edge - lower_edge)
    ratio_sigma = centre / radius
    previous_rho = 1.0 / ratio_sigma
    weights = []
    for turn_index in range(SWEEPS - 1):
        current_rho = 1.0 / (2.0 * ratio_sigma - previous_rho)
        weights.append((current_rho * previous_rho, 2.0 * current_rho / radius))
        previous_rho = current_rho
    return (centre, weights)


def two_parts(x):
    high = x.astype(jnp.bfloat16)
    low = (x - high.astype(jnp.float32)).astype(jnp.bfloat16)
    return [high, low]


def stencil_matrix():
    source = lax.broadcasted_iota(jnp.int32, (2 * LANES, 2 * LANES), 0) % LANES
    column = lax.broadcasted_iota(jnp.int32, (2 * LANES, 2 * LANES), 1)
    target = column % LANES
    gap = jnp.abs(source - target)
    same = (source // B) == (target // B)
    inside = jnp.where(
        same,
        jnp.where(gap == 0, 90.0, jnp.where(gap == 1, -16.0, jnp.where(gap == 2, 1.0, 0.0))),
        jnp.where(gap == B, -16.0, 0.0),
    )
    across = jnp.where(gap == B, -16.0, 0.0)
    return jnp.where(column < LANES, inside, across).astype(jnp.bfloat16)


def operator12(window, matrix, count):
    rows = count * PLANE_ROWS

    def planes(start):
        return window[start : start + count].reshape(rows, LANES)

    x = planes(2)
    product = jnp.dot(
        jnp.concatenate(two_parts(x), axis=1), matrix, preferred_element_type=jnp.float32
    )
    inside, across = product[:, :LANES], product[:, LANES:]
    lane = lax.broadcasted_iota(jnp.int32, (rows, LANES), 1)
    row = lax.broadcasted_iota(jnp.int32, (rows, LANES), 0) % PLANE_ROWS
    downward = x + jnp.where(lane < B, across, 0.0)
    upward = x + jnp.where(lane >= B, across, 0.0)
    downward = jnp.where(row == 0, 0.0, pltpu.roll(downward, 1, 0))
    upward = jnp.where(row == PLANE_ROWS - 1, 0.0, pltpu.roll(upward, rows - 1, 0))
    beside = planes(0) + planes(4) - 16.0 * (planes(1) + planes(3))
    return inside + downward + upward + beside


def shift_matrix(odd, across):
    shape = (LANES, LANES)
    source = lax.broadcasted_iota(jnp.int32, shape, 0)
    target = lax.broadcasted_iota(jnp.int32, shape, 1)
    cells = (source % B) == (target % B) + across
    half = target // B + odd - source // B

    def one(wanted):
        return jnp.where(cells & (half == wanted), 1.0, 0.0).astype(jnp.bfloat16)

    here, following = one(0), one(2)
    return jnp.concatenate([here, here, following, following], axis=0)


def shifted(padded, first, offset, matrix):
    plane = SHIFT + first + offset[0]
    row = ROW_PAD + (offset[1] >> 1)
    rows = CHUNK * PLANE_ROWS
    here = padded[pl.ds(plane, CHUNK), pl.ds(row, PLANE_ROWS), :].reshape(rows, LANES)
    following = padded[pl.ds(plane, CHUNK), pl.ds(row + 1, PLANE_ROWS), :].reshape(rows, LANES)
    parts = jnp.concatenate(two_parts(here) + two_parts(following), axis=1)
    return jnp.dot(parts, matrix, preferred_element_type=jnp.float32)


def pair_kernel(
    chosen, offsets, mine, theirs, kept, passed,
    padded, own, moved, first, second, residual, total, own_force, stencil, mover,
):
    chips, _, depth = mine.shape[:3]
    core = lax.rem(lax.axis_index("grid"), CORES)
    base = core
    if mine.shape[1] > theirs.shape[1]:
        base = lax.axis_index("grid")
    chunks = B // CHUNK
    centre, weights = sweep_weights()
    shape3 = (CHUNK, PLANE_ROWS, LANES)

    stencil[...] = stencil_matrix()
    zero_plane = jnp.zeros((2, PLANE_ROWS, LANES), jnp.float32)
    for buffer in (first, second):
        buffer[0:2] = zero_plane
        buffer[B + 2 : B + 4] = zero_plane
    own_force[...] = jnp.zeros_like(own_force)
    kept[...] = jnp.zeros_like(kept)
    passed[...] = jnp.zeros_like(passed)

    @pl.loop(0, padded.shape[0])
    def _(plane):
        padded[plane] = jnp.zeros(padded.shape[1:], jnp.float32)

    def slab_start(chip, which):
        return (chip * CORES + which) * depth

    @pl.loop(0, chips)
    def _(chip):
        own[pl.ds(slab_start(chip, core), depth)] = mine[chip, base]
        own[pl.ds(slab_start(chip, 1 - core), depth)] = theirs[chip, core]

    @pl.loop(0, chosen.shape[0])
    def _(pair):
        partner = chosen[pair]
        offset = [offsets[pair, axis] for axis in range(3)]
        inside_rows = pl.ds(ROW_PAD, PLANE_ROWS)

        @pl.loop(0, chips)
        def _(chip):
            padded[pl.ds(SHIFT + slab_start(chip, core), depth), inside_rows, :] = mine[
                chip, base + partner
            ]
            padded[pl.ds(SHIFT + slab_start(chip, 1 - core), depth), inside_rows, :] = theirs[
                chip, core + partner
            ]

        mover[...] = shift_matrix(offset[1] & 1, offset[2])

        @pl.loop(0, chunks)
        def _(chunk):
            at = pl.multiple_of(chunk * CHUNK, CHUNK)
            there = shifted(padded, at, offset, mover[...]).reshape(shape3)
            moved[pl.ds(at, CHUNK)] = there
            start = coulomb_factor * (own[pl.ds(at, CHUNK)] * there)
            residual[pl.ds(at, CHUNK)] = start
            direction = start * (1.0 / centre)
            first[pl.ds(at + 2, CHUNK)] = direction
            total[pl.ds(at, CHUNK)] = direction

        source, target = first, second
        for turn in range(SWEEPS - 1):
            keep_weight, residual_weight = weights[turn]
            last = turn == SWEEPS - 2

            @pl.loop(0, chunks)
            def _(chunk, source=source, target=target, keep=keep_weight, gain=residual_weight, last=last):
                at = pl.multiple_of(chunk * CHUNK, CHUNK)
                window = source[pl.ds(at, CHUNK + 4)]
                applied = operator12(window, stencil[...], CHUNK).reshape(shape3)
                left = residual[pl.ds(at, CHUNK)] - (1.0 / 12.0) * applied
                direction = keep * window[2 : CHUNK + 2] + gain * left
                solved = total[pl.ds(at, CHUNK)] + direction
                if last:
                    own_force[pl.ds(at, CHUNK)] += solved * moved[pl.ds(at, CHUNK)]
                    padded[pl.ds(SHIFT + at, CHUNK), inside_rows, :] = solved * own[pl.ds(at, CHUNK)]
                else:
                    residual[pl.ds(at, CHUNK)] = left
                    target[pl.ds(at + 2, CHUNK)] = direction
                    total[pl.ds(at, CHUNK)] = solved

            source, target = target, source

        back = [-part for part in offset]
        mover[...] = shift_matrix(back[1] & 1, back[2])

        @pl.loop(0, chunks)
        def _(chunk):
            at = pl.multiple_of(chunk * CHUNK, CHUNK)
            there = shifted(padded, at, back, mover[...]).reshape(shape3)
            total[pl.ds(at, CHUNK)] = exact_share * there

        @pl.loop(0, chips)
        def _(chip):
            kept[chip, core + partner] = total[pl.ds(slab_start(chip, core), depth)]
            passed[chip, core + partner] = total[pl.ds(slab_start(chip, 1 - core), depth)]

    @pl.loop(0, chips)
    def _(chip):
        kept[chip, core] = exact_share * own_force[pl.ds(slab_start(chip, core), depth)]
        passed[chip, core] = exact_share * own_force[pl.ds(slab_start(chip, 1 - core), depth)]


def pair_forces(chosen, offsets, mine, theirs):
    box = (B, PLANE_ROWS, LANES)
    f32 = jnp.float32
    vmem = pl.BlockSpec(memory_space=pltpu.VMEM)
    smem = pl.BlockSpec(memory_space=pltpu.SMEM)
    return pl.pallas_call(
        pair_kernel,
        out_shape=(
            jax.ShapeDtypeStruct(theirs.shape, f32),
            jax.ShapeDtypeStruct(theirs.shape, f32),
        ),
        in_specs=[smem, smem, vmem, vmem],
        out_specs=(vmem, vmem),
        scratch_shapes=[
            pltpu.VMEM((B + 2 * SHIFT, PADDED_ROWS, LANES), f32),
            pltpu.VMEM(box, f32),
            pltpu.VMEM(box, f32),
            pltpu.VMEM((B + 4, PLANE_ROWS, LANES), f32),
            pltpu.VMEM((B + 4, PLANE_ROWS, LANES), f32),
            pltpu.VMEM(box, f32),
            pltpu.VMEM(box, f32),
            pltpu.VMEM(box, f32),
            pltpu.VMEM((2 * LANES, 2 * LANES), jnp.bfloat16),
            pltpu.VMEM((4 * LANES, LANES), jnp.bfloat16),
        ],
        compiler_params=pltpu.CompilerParams(vmem_limit_bytes=36 << 20),
        name="pair_forces",
    )(chosen, offsets, mine, theirs)


def step_kernel(now, before, after, previous, potential, partial, stencil):
    @pl.when(pl.program_id(0) == 0)
    def _():
        stencil[...] = stencil_matrix()

    depth = now.shape[1]
    window = jnp.concatenate([before[0], now[0], after[0]], axis=0)
    applied = operator12(window, stencil[...], depth)
    kinetic = (-0.5 / 12.0) * applied.reshape(now.shape[1:])
    field = now[0]
    partial[0] = (
        2.0 * field - previous[0] + verlet_factor * (kinetic - potential[0] * field)
    )


def step_without_force(now, before, after, previous, potential):
    count = now.shape[0]

    def spec(array):
        return pl.BlockSpec((1,) + array.shape[1:], lambda n: (n, 0, 0, 0))

    operands = (now, before, after, previous, potential)
    return pl.pallas_call(
        step_kernel,
        grid=(count,),
        out_shape=jax.ShapeDtypeStruct(now.shape, jnp.float32),
        in_specs=[spec(array) for array in operands],
        out_specs=spec(now),
        scratch_shapes=[pltpu.VMEM((2 * LANES, 2 * LANES), jnp.bfloat16)],
        cost_estimate=pl.CostEstimate(
            flops=40 * now.size, bytes_accessed=20 * now.size, transcendentals=0
        ),
        compiler_params=pltpu.CompilerParams(vmem_limit_bytes=12 << 20),
        name="step_without_force",
    )(*operands)


LINK_TIME = 5.6
HOP_TIME = 2.0
UPPER_TIME = 12.0


def arrival_orders(chips, steps, gathering):
    items = chips + steps
    pending, orders, free = [], [[] for _ in range(chips)], {}
    for chip in range(chips):
        for flow in (1, -1):
            for s in range(chips):
                for k in range(items):
                    if gathering:
                        starts = s == chip
                        last = min(k, chips - 1) if flow > 0 else max(0, k - steps)
                        hops = (last - chip) * flow
                        ready = 0.0 if k < chips else UPPER_TIME
                    else:
                        hops = (s - chip) * flow
                        alone = k == chip + steps if flow > 0 else k == chip
                        edge = chip == 0 if flow > 0 else chip == chips - 1
                        starts = chip <= k <= chip + steps and (alone or edge)
                        ready = 1.0
                    if starts and hops > 0:
                        pending.append((ready, -hops, chip, flow, s, k, hops))
    while pending:
        pending.sort()
        ready, _, chip, flow, s, k, hops = pending.pop(0)
        orders[chip].append((ready, flow, s, k))
        if hops > 0:
            sent = max(ready, free.get((chip, flow), 0.0)) + LINK_TIME
            free[chip, flow] = sent
            pending.append((sent + HOP_TIME, 1 - hops, chip + flow, flow, s, k, hops - 1))
    return orders


def position():
    orb, grid = lax.axis_index("orb"), lax.axis_index("grid")
    return orb, grid, grid // CORES, lax.rem(grid, CORES)


def greet(devices):
    barrier = pltpu.get_barrier_semaphore()
    for there, device in devices:

        @pl.when(there)
        def _(device=device):
            pl.semaphore_signal(barrier, inc=1, device_id=device, device_id_type=MESH)

    pl.semaphore_wait(barrier, sum(there.astype(jnp.int32) for there, _ in devices))


def gather_kernel(
    planes, held, other, local_sem, up_send, right_send, left_send, recv, swap_send, swap_recv
):
    chips, items = held.shape[:2]
    steps = items - chips
    orb, grid, chip, core = position()
    orbs = lax.axis_size("orb")
    sibling = (orb, grid + 1 - 2 * core)
    right, left = (orb, grid + CORES), (orb, grid - CORES)
    up, down = (lax.rem(orb + 1, orbs), grid), (lax.rem(orb + orbs - 1, orbs), grid)
    has_right, has_left, always = chip < chips - 1, chip > 0, chip >= 0
    greet([(always, sibling), (has_right, right), (has_left, left), (always, up), (always, down)])

    def remote(source, target, sent, landed, device):
        return pltpu.make_async_remote_copy(
            src_ref=source, dst_ref=target, send_sem=sent, recv_sem=landed,
            device_id=device, device_id_type=MESH,
        )

    def upward(j):
        k = chips + j
        return remote(planes.at[j], held.at[chip, k], up_send.at[j], recv.at[chip, k], down)

    def rightward(s, k, source):
        return remote(source, held.at[s, k], right_send.at[s, k], recv.at[s, k], right)

    def leftward(s, k, source):
        return remote(source, held.at[s, k], left_send.at[s, k], recv.at[s, k], left)

    def across(s, j, source):
        return remote(source, other.at[s, j], swap_send.at[s, j], swap_recv.at[s, j], sibling)

    def goes_right(k):
        return has_right & (k >= chip + 1)

    def goes_left(k):
        return has_left & (k <= chip - 1 + steps)

    def wanted(k):
        return (k >= chip) & (k <= chip + steps)

    for j in range(steps):
        upward(j).start()
    keep = pltpu.make_async_copy(planes, held.at[chip, pl.ds(0, chips)], local_sem)
    keep.start()

    for here, order in enumerate(arrival_orders(chips, steps, True)):

        @pl.when(chip == here)
        def _(here=here, order=order):
            arrived, swapped = set(), set()
            for _, flow, slab, k in order:
                own = slab == here
                item = planes.at[k] if own and k < chips else held.at[slab, k]
                send = rightward if flow > 0 else leftward
                if own and k >= chips and k not in arrived:
                    upward(k - chips).wait_recv()
                    arrived.add(k)
                if not own:
                    send(slab, k, item).wait_recv()
                onward = here + 1 <= min(k, chips - 1) if flow > 0 else here - 1 >= max(0, k - steps)
                if onward:
                    send(slab, k, item).start()
                if here <= k <= here + steps and (slab, k) not in swapped:
                    across(slab, k - here, item).start()
                    swapped.add((slab, k))
            for k in range(chips, items):
                if k not in arrived:
                    upward(k - chips).wait_recv()
            for k in range(here, here + steps + 1):
                if (here, k) not in swapped:
                    across(here, k - here, planes.at[k] if k < chips else held.at[here, k]).start()

    keep.wait()
    for j in range(steps):
        upward(j).wait_send()

    @pl.loop(0, chips)
    def _(s):
        @pl.loop(0, items)
        def _(k):
            item = planes.at[0]

            @pl.when(goes_right(k) & (s <= chip))
            def _():
                rightward(s, k, item).wait_send()

            @pl.when(goes_left(k) & (s >= chip))
            def _():
                leftward(s, k, item).wait_send()

        @pl.loop(0, steps + 1)
        def _(j):
            across(s, j, planes.at[0]).wait()


def gather_boxes(planes, steps):
    chips = planes.shape[0]
    items = chips + steps
    tail = planes.shape[1:]
    anywhere = pl.BlockSpec(memory_space=pl.ANY)
    dma = pltpu.SemaphoreType.DMA
    return pl.pallas_call(
        gather_kernel,
        out_shape=(
            jax.ShapeDtypeStruct((chips, items) + tail, planes.dtype),
            jax.ShapeDtypeStruct((chips, steps + 1) + tail, planes.dtype),
        ),
        in_specs=[pl.BlockSpec(memory_space=pltpu.VMEM)],
        out_specs=(anywhere, anywhere),
        scratch_shapes=[
            dma, dma((steps,)), dma((chips, items)), dma((chips, items)), dma((chips, items)),
            dma((chips, steps + 1)), dma((chips, steps + 1)),
        ],
        compiler_params=pltpu.CompilerParams(
            collective_id=0, has_side_effects=True, vmem_limit_bytes=8 << 20
        ),
        name="gather_boxes",
    )(planes)


def return_kernel(
    kept, passed, folded, sibling_in, left_in, right_in,
    swap_send, swap_recv, left_send, left_recv, right_send, right_recv,
):
    chips, items = left_in.shape[:2]
    steps = items - chips
    orb, grid, chip, core = position()
    sibling = (orb, grid + 1 - 2 * core)
    right, left = (orb, grid + CORES), (orb, grid - CORES)
    has_right, has_left, always = chip < chips - 1, chip > 0, chip >= 0
    greet([(always, sibling), (has_right, right), (has_left, left)])

    def remote(source, target, sent, landed, device):
        return pltpu.make_async_remote_copy(
            src_ref=source, dst_ref=target, send_sem=sent, recv_sem=landed,
            device_id=device, device_id_type=MESH,
        )

    def across(s, j):
        return remote(
            passed.at[s, j], sibling_in.at[s, j], swap_send.at[s, j], swap_recv.at[s, j], sibling
        )

    def leftward(s, k):
        return remote(
            left_in.at[s, k], left_in.at[s, k], left_send.at[s, k], left_recv.at[s, k], left
        )

    def rightward(s, k):
        return remote(
            right_in.at[s, k], right_in.at[s, k], right_send.at[s, k], right_recv.at[s, k], right
        )

    def from_right(k):
        return has_right & (k >= chip + 1)

    def from_left(k):
        return has_left & (k <= chip - 1 + steps)

    def contributes(k):
        return (k >= chip) & (k <= chip + steps)

    def share(s, k):
        return kept[s, k - chip] + sibling_in[s, k - chip]

    for turn in range(chips):
        for s, leaves in ((turn, chip > turn), (chips - 1 - turn, chip < chips - 1 - turn)):

            @pl.loop(0, steps + 1)
            def _(j, s=s, leaves=leaves):
                @pl.when(leaves)
                def _():
                    across(s, j).start()

    @pl.loop(0, steps + 1)
    def _(j):
        across(chip, j).start()

    for here, order in enumerate(arrival_orders(chips, steps, False)):

        @pl.when(chip == here)
        def _(here=here, order=order):
            swapped = set()
            for _, flow, slab, k in order:
                if slab == here:
                    continue
                buffer, send = (right_in, rightward) if flow > 0 else (left_in, leftward)
                alone = (here == 0 or k == here + steps) if flow > 0 else (here == chips - 1 or k == here)
                if not alone:
                    send(slab, k).wait_recv()
                if here <= k <= here + steps:
                    if (slab, k) not in swapped:
                        across(slab, k - here).wait_recv()
                        swapped.add((slab, k))
                    added = kept[slab, k - here] + sibling_in[slab, k - here]
                    buffer[slab, k] = added if alone else buffer[slab, k] + added
                send(slab, k).start()

    @pl.loop(0, items)
    def _(k):
        folded[k] = jnp.zeros(folded.shape[1:], folded.dtype)

        @pl.when(contributes(k))
        def _():
            across(chip, k - chip).wait_recv()
            folded[k] = share(chip, k)

        @pl.when(from_right(k))
        def _():
            leftward(chip, k).wait_recv()
            folded[k] += left_in[chip, k]

        @pl.when(from_left(k))
        def _():
            rightward(chip, k).wait_recv()
            folded[k] += right_in[chip, k]

    @pl.loop(0, chips)
    def _(s):
        @pl.loop(0, steps + 1)
        def _(j):
            across(s, j).wait_send()

        @pl.loop(0, items)
        def _(k):
            @pl.when((s < chip) & (k >= chip))
            def _():
                leftward(s, k).wait_send()

            @pl.when((s > chip) & (k <= chip + steps))
            def _():
                rightward(s, k).wait_send()


def return_forces(kept, passed):
    chips, span = kept.shape[:2]
    items = chips + span - 1
    tail = kept.shape[2:]
    vmem = pl.BlockSpec(memory_space=pltpu.VMEM)
    dma = pltpu.SemaphoreType.DMA
    line = (chips, items)
    return pl.pallas_call(
        return_kernel,
        out_shape=jax.ShapeDtypeStruct((items,) + tail, kept.dtype),
        in_specs=[vmem, vmem],
        out_specs=vmem,
        scratch_shapes=[
            pltpu.VMEM(kept.shape, kept.dtype),
            pltpu.VMEM(line + tail, kept.dtype),
            pltpu.VMEM(line + tail, kept.dtype),
            dma((chips, span)), dma((chips, span)), dma(line), dma(line), dma(line), dma(line),
        ],
        compiler_params=pltpu.CompilerParams(
            collective_id=1, has_side_effects=True, vmem_limit_bytes=26 << 20
        ),
        name="return_forces",
    )(kept, passed)


def from_behind(array, axis, by):
    count = lax.axis_size(axis)
    return lax.ppermute(array, axis, [(i, (i + by) % count) for i in range(count)])


def neighbour_planes(planes):
    count = lax.axis_size("grid")
    depth = planes.shape[1]
    before, after = [], []
    for hop in range(1, -(-2 // depth) + 1):
        size = min(depth, 2 - (hop - 1) * depth)
        forward = [(i, i + hop) for i in range(count - hop)]
        backward = [(i + hop, i) for i in range(count - hop)]
        before.insert(0, lax.ppermute(planes[:, depth - size :], "grid", forward))
        after.append(lax.ppermute(planes[:, :size], "grid", backward))
    return jnp.concatenate(before, axis=1), jnp.concatenate(after, axis=1)


def local(orbitals, previous, potential, partners, offsets):
    slabs = lax.axis_size("grid")
    chips = slabs // CORES
    total_orbitals = lax.axis_size(("orb", "grid"))
    group, rows, width = orbitals.shape
    depth = rows // PLANE_ROWS
    planes = orbitals.reshape(group, depth, PLANE_ROWS, width)
    tail = planes.shape[1:]
    steps = AHEAD // CORES
    across = [[chip * CORES + c for chip in range(chips)] for c in range(CORES)]
    swap = [(i, i + 1 - 2 * (i % CORES)) for i in range(slabs)]

    before, after = neighbour_planes(planes)
    by_chip = (chips, CORES) + tail
    boxes = (CORES * (steps + 1),) + tail
    relayed = chips * (chips + steps) <= RELAY_ITEMS

    def exchange(array):
        return lax.all_to_all(
            array, "grid", split_axis=0, concat_axis=0, axis_index_groups=across, tiled=True
        )

    if relayed:
        mine, theirs = gather_boxes(planes.reshape(by_chip), steps)
        mine = mine.reshape((chips, CORES * (chips + steps)) + tail)
        theirs = theirs.reshape((chips,) + boxes)
    else:
        upper = from_behind(planes[:AHEAD], "orb", -1)
        blocks = jnp.concatenate([planes, upper], axis=0).reshape((chips + steps, CORES) + tail)
        own_group = exchange(planes.reshape(by_chip))
        ahead = exchange(
            jnp.concatenate([blocks[s : s + chips] for s in range(1, steps + 1)], axis=1)
        )
        mine = jnp.concatenate([own_group, ahead], axis=1)
        theirs = lax.ppermute(mine, "grid", swap)

    first_index = lax.axis_index(("orb", "grid"))
    chosen = jnp.remainder(partners - first_index, total_orbitals).reshape(-1)
    partial = step_without_force(
        planes, before, after, previous.reshape(planes.shape), potential.reshape(planes.shape)
    )
    chosen, partial = lax.optimization_barrier((chosen, partial))
    kept, passed = pair_forces(chosen, offsets[0], mine, theirs)

    if relayed:
        pairs = (chips, steps + 1, CORES) + tail
        folded = return_forces(kept.reshape(pairs), passed.reshape(pairs))
    else:
        summed = kept + lax.ppermute(passed, "grid", swap)
        returned = exchange(summed).reshape((chips, steps + 1, CORES) + tail)
        folded = sum(
            jnp.pad(returned[:, s], ((s, steps - s),) + ((0, 0),) * (len(tail) + 1))
            for s in range(steps + 1)
        )
    folded = folded.reshape(((chips + steps) * CORES,) + tail)
    spilled = from_behind(folded[group:], "orb", 1)
    force = folded[:group] + jnp.pad(spilled, ((0, group - AHEAD),) + ((0, 0),) * len(tail))

    advanced = partial + verlet_factor * force
    return advanced.reshape(orbitals.shape), force.reshape(orbitals.shape)


def solution(mesh):
    in_specs = (
        P("orb", "grid", None),
        P("orb", "grid", None),
        P("orb", "grid", None),
        P(("orb", "grid"), None),
        P(("orb", "grid"), None, None),
    )
    out_specs = (P("orb", "grid", None), P("orb", "grid", None))
    return jax.shard_map(local, mesh=mesh, in_specs=in_specs, out_specs=out_specs, check_vma=False)
```
